32 devices in a mesh: req: 2 (over y), ctx: 16 (over z, x, core).
Axes of the slice: x: 2, y: 2, z: 4, core: 2. Of those that a mesh axis runs over, the one named last changes fastest.
Arguments:
- query_source: bfloat16 [2304, 256], P(('req', 'ctx')), parts along dimension 0, may hold values from -32 to 32
- key_source: bfloat16 [2304, 256], P(('req', 'ctx')), parts along dimension 0, may hold values from -4 to 4
- query_edit: bfloat16 [2304, 256], P(('req', 'ctx')), parts along dimension 0, may hold values from -32 to 32
- key_edit: bfloat16 [2304, 256], P(('req', 'ctx')), parts along dimension 0, may hold values from -4 to 4
- text_count: int32 [2], P('req'), parts along dimension 0, may hold values from 72 to 288, as said below
Outputs:
- query_grad: float32 [2304, 256], P(('req', 'ctx')), parts along dimension 0
- key_grad: float32 [2304, 256], P(('req', 'ctx')), parts along dimension 0
The draws below stay inside these ranges and needn't reach their ends.
There are 2 independent parts, one for each index of `req`. The reference program is written for one: setup_inputs(seed, part) draws one part's arguments, and reference() takes and returns one part's arrays. A program takes and returns all parts, laid end to end along the dimension named above; each array names one. Nothing has to cross between parts.
Inputs may be any that keep to these rules, and one draw needn't show every extreme that they name: The first 288 positions are text slots; those at or past text_count are padding.
All inputs are finite; a program needn't handle non-finite values.
Results may differ from the reference program's by a relative error of at most 0.0095.
Values may be sent and summed in bfloat16 or wider, within the bound.
A program may use at most 64 MiB of HBM per device.

```python
import math
import jax
import jax.numpy as jnp
from jax import lax

HEADS = 2
HEAD_DIM = 128
TOKENS = 1152
TEXT = 288


def draw_pair(key, offset_salt):
    base_key = jax.random.fold_in(key, offset_salt)
    first_key, second_key = jax.random.split(base_key)
    full_shape = (TOKENS, HEADS, HEAD_DIM)
    keys_all = jnp.clip(jax.random.normal(first_key, full_shape, jnp.float32), -4.0, 4.0)
    queries = jnp.clip(jax.random.normal(second_key, full_shape, jnp.float32), -4.0, 4.0)
    return (queries.reshape(TOKENS, HEADS * HEAD_DIM), keys_all.reshape(TOKENS, HEADS * HEAD_DIM))


def draw_query_source(key, part):
    return draw_pair(key, 101)[0].astype(jnp.bfloat16)


def draw_key_source(key, part):
    return draw_pair(key, 101)[1].astype(jnp.bfloat16)


def draw_query_edit(key, part):
    return draw_pair(key, 202)[0].astype(jnp.bfloat16)


def draw_key_edit(key, part):
    return draw_pair(key, 202)[1].astype(jnp.bfloat16)


def draw_text_count(key, part):
    lowest = TEXT // 4
    picked = jax.random.randint(jax.random.fold_in(key, 303), (1,), lowest, TEXT, jnp.int32)
    parity = jnp.asarray(part, jnp.int32) % 2
    return jnp.where(parity == 1, jnp.full((1,), TEXT, jnp.int32), picked).astype(jnp.int32)


def setup_inputs(seed: int = 0, part: int = 0) -> dict:
    splits = jax.random.split(jax.random.key(seed), 6)
    part_keys = jax.random.split(jax.random.fold_in(splits[5], part), 6)
    return {
        "query_source": draw_query_source(jax.random.fold_in(jax.random.fold_in(splits[5], part), 71), part),
        "key_source": draw_key_source(jax.random.fold_in(jax.random.fold_in(splits[5], part), 71), part),
        "query_edit": draw_query_edit(jax.random.fold_in(jax.random.fold_in(splits[5], part), 71), part),
        "key_edit": draw_key_edit(jax.random.fold_in(jax.random.fold_in(splits[5], part), 71), part),
        "text_count": draw_text_count(jax.random.fold_in(jax.random.fold_in(splits[5], part), 71), part),
    }


def masked_probs(scores, key_valid):
    masked = jnp.where(key_valid, scores, -jnp.inf)
    highest = lax.optimization_barrier(jnp.max(masked, axis=-1, keepdims=True))
    powers = jnp.where(key_valid, jnp.exp(scores - highest), 0.0)
    return powers / lax.optimization_barrier(jnp.sum(powers, axis=-1, keepdims=True))

def reference(query_source, key_source, query_edit, key_edit, text_count):
    score_scale = 1.0 / math.sqrt(HEAD_DIM)
    weight = 4.0 * TOKENS * math.sqrt(TOKENS)
    places = jnp.arange(TOKENS)
    token_valid = (places >= TEXT) | (places < text_count[0])
    row_weight = token_valid.astype(jnp.float32)
    block_rows = TOKENS // 8

    def split_heads(matrix):
        return matrix.reshape(TOKENS, HEADS, HEAD_DIM).transpose(1, 0, 2)

    def per_head(inputs):
        head_qs, head_ks, head_qe, head_ke = inputs
        blocks_qs = head_qs.reshape(8, block_rows, HEAD_DIM)
        blocks_qe = head_qe.reshape(8, block_rows, HEAD_DIM)
        blocks_weight = row_weight.reshape(8, block_rows, 1)

        def per_block(carry, block):
            block_qs, block_qe, block_weight = block
            scores_source = jnp.dot(block_qs, head_ks.T, preferred_element_type=jnp.float32) * score_scale
            scores_edit = jnp.dot(block_qe, head_ke.T, preferred_element_type=jnp.float32) * score_scale
            probs_source = masked_probs(scores_source, token_valid[None, :])
            probs_edit = masked_probs(scores_edit, token_valid[None, :])
            map_grad = 2.0 * weight * (probs_edit - probs_source) * block_weight
            row_delta = lax.optimization_barrier(jnp.sum(map_grad * probs_edit, axis=1, keepdims=True))
            score_grad = (probs_edit * (map_grad - row_delta)).astype(jnp.bfloat16)
            block_qgrad = jnp.dot(score_grad, head_ke, preferred_element_type=jnp.float32) * score_scale
            block_kgrad = jnp.dot(score_grad.T, block_qe, preferred_element_type=jnp.float32) * score_scale
            return (carry + block_kgrad, block_qgrad)
        start_grad = jnp.zeros((TOKENS, HEAD_DIM), jnp.float32)
        head_kgrad, head_qgrad = lax.scan(per_block, start_grad, (blocks_qs, blocks_qe, blocks_weight))
        return (head_qgrad.reshape(TOKENS, HEAD_DIM), head_kgrad)
    query_grads, key_grads = lax.map(per_head, (split_heads(query_source), split_heads(key_source), split_heads(query_edit), split_heads(key_edit)))
    query_grad = query_grads.transpose(1, 0, 2).reshape(TOKENS, HEADS * HEAD_DIM)
    key_grad = key_grads.transpose(1, 0, 2).reshape(TOKENS, HEADS * HEAD_DIM)
    return (query_grad, key_grad)
```

```python
import functools
import math

import jax
import jax.numpy as jnp
from jax import lax
from jax.experimental import pallas as pl
from jax.experimental.pallas import tpu as pltpu
from jax.sharding import PartitionSpec as P

HEAD_DIM = 128
MASKED = -1e30
SQUARE = False
F32 = jnp.float32
BF16 = jnp.bfloat16


def kernel(
    chips,
    count_ref, qs_hbm, ks_hbm, qe_hbm, ke_hbm,
    qg_ref, kg_ref,
    krecv, kother, qrecv, qother, e_buf, s_buf, m_buf, st_send, st_recv,
    kg_send, kg_recv, qg_send, qg_recv, kg_own, qg_own,
    load_sem, ksend_sem, krecv_sem, qsend_sem, qrecv_sem, st_sems,
    kgsend_sem, kgrecv_sem, qgsend_sem, qgrecv_sem,
):
    members = chips // 2
    rows = krecv.shape[3]
    all_rows = rows * chips * 2
    text_slots = min(512, all_rows // 4)
    scale = 1.0 / math.sqrt(HEAD_DIM)
    weight = 4.0 * all_rows * math.sqrt(all_rows)
    me = lax.axis_index("ctx")
    chip, core = me // 2, me % 2
    other = 1 - core

    if SQUARE:
        group, member = chip // members, chip % members
        chip_of = lambda g, m: g * members + m
    else:
        group, member = chip % 2, chip // 2
        chip_of = lambda g, m: m * 2 + g

    def dev(g, m, c):
        return {"ctx": chip_of(g, m) * 2 + c}

    def shifted(d):
        return (member + d) % members

    def each(n, body, init):
        if n <= 8:
            for i in range(n):
                init = body(i, init)
            return init
        return lax.fori_loop(0, n, body, init)

    own_cols = pl.ds(pl.multiple_of(core * HEAD_DIM, HEAD_DIM), HEAD_DIM)
    other_cols = pl.ds(pl.multiple_of(other * HEAD_DIM, HEAD_DIM), HEAD_DIM)
    loads = []
    for i, (src, dst_own, dst_other) in enumerate((
        (ks_hbm, krecv.at[member, core, 0], kother.at[0]),
        (ke_hbm, krecv.at[member, core, 1], kother.at[1]),
        (qs_hbm, qrecv.at[group, core, 0], qother.at[0]),
        (qe_hbm, qrecv.at[group, core, 1], qother.at[1]),
    )):
        loads.append(pltpu.make_async_copy(src.at[:, own_cols], dst_own, load_sem.at[2 * i]))
        loads.append(pltpu.make_async_copy(src.at[:, other_cols], dst_other, load_sem.at[2 * i + 1]))
    for load in loads:
        load.start()

    barrier = pltpu.get_barrier_semaphore()

    def greet(d, carry):
        for c in (0, 1):
            pl.semaphore_signal(barrier, inc=1, device_id=dev(group, shifted(d + 1), c))
        return carry

    for c in (0, 1):
        pl.semaphore_signal(barrier, inc=1, device_id=dev(1 - group, member, c))
    pl.semaphore_signal(barrier, inc=1, device_id=dev(group, member, other))
    each(members - 1, greet, 0)
    pl.semaphore_wait(barrier, 2 * members + 1)
    for load in loads:
        load.wait()

    def key_copy(m, c, same):
        return pltpu.make_async_remote_copy(
            src_ref=krecv.at[member, core] if same else kother,
            dst_ref=krecv.at[member, core],
            send_sem=ksend_sem.at[m, c],
            recv_sem=krecv_sem.at[member, core],
            device_id=dev(group, m, c),
        )

    def key_arrival(m, c):
        return pltpu.make_async_remote_copy(
            src_ref=kother,
            dst_ref=krecv.at[m, c],
            send_sem=ksend_sem.at[m, c],
            recv_sem=krecv_sem.at[m, c],
            device_id=dev(group, m, c),
        )

    def query_copy(g, c, same):
        return pltpu.make_async_remote_copy(
            src_ref=qrecv.at[group, core] if same else qother,
            dst_ref=qrecv.at[group, core],
            send_sem=qsend_sem.at[g, c],
            recv_sem=qrecv_sem.at[group, core],
            device_id=dev(g, member, c),
        )

    def query_arrival(g, c):
        return pltpu.make_async_remote_copy(
            src_ref=qother,
            dst_ref=qrecv.at[g, c],
            send_sem=qsend_sem.at[g, c],
            recv_sem=qrecv_sem.at[g, c],
            device_id=dev(g, member, c),
        )

    query_copy(1 - group, core, True).start()
    query_copy(1 - group, other, False).start()
    query_copy(group, other, False).start()
    key_copy(member, other, False).start()

    def send_keys(d, carry):
        m = shifted(d + 1)
        key_copy(m, core, True).start()
        key_copy(m, other, False).start()
        return carry

    each(members - 1, send_keys, 0)

    count = count_ref[0]

    def valid(positions):
        return (positions >= text_slots) | (positions < count)

    query_arrival(group, other).wait_recv()
    query_arrival(1 - group, core).wait_recv()
    query_arrival(1 - group, other).wait_recv()

    def queries(which):
        pieces = [qrecv[g, c, which].astype(F32) for g in (0, 1) for c in (0, 1)]
        return jnp.concatenate(pieces, axis=0).astype(BF16)

    q_source, q_edit = queries(0), queries(1)
    width = 4 * rows
    lane = lax.broadcasted_iota(jnp.int32, (1, width), 1)
    piece = lane // rows
    lane_chip = jnp.where(piece < 2, chip_of(0, member), chip_of(1, member))
    row_place = (lane_chip * 2 + piece % 2) * rows + lane % rows
    row_weight = jnp.where(valid(row_place), 2.0 * weight, 0.0)

    def keys(m, which):
        pieces = [krecv[m, c, which].astype(F32) for c in (0, 1)]
        return jnp.concatenate(pieces, axis=0).astype(BF16)

    def merge(a, b):
        me1, le1, ms1, ls1, sq1, cr1 = a
        me2, le2, ms2, ls2, sq2, cr2 = b
        m_e, m_s = jnp.maximum(me1, me2), jnp.maximum(ms1, ms2)
        fe1, fe2 = jnp.exp(me1 - m_e), jnp.exp(me2 - m_e)
        fs1, fs2 = jnp.exp(ms1 - m_s), jnp.exp(ms2 - m_s)
        return (
            m_e, le1 * fe1 + le2 * fe2,
            m_s, ls1 * fs1 + ls2 * fs2,
            sq1 * fe1 * fe1 + sq2 * fe2 * fe2,
            cr1 * fe1 * fs1 + cr2 * fe2 * fs2,
        )

    def powers(m, which, q, key_valid, buf):
        scores = lax.dot_general(
            keys(m, which), q, (((1,), (1,)), ((), ())), preferred_element_type=F32
        ) * scale
        scores = jnp.where(key_valid, scores, MASKED)
        top = jnp.max(scores, axis=0, keepdims=True)
        power = jnp.where(key_valid, jnp.exp(scores - top), 0.0)
        buf[m] = power
        m_buf[m, which:which + 1] = top
        return top, power, jnp.sum(power, axis=0, keepdims=True)

    def score_chunk(m, stats):
        place = chip_of(group, m) * (2 * rows) + lax.broadcasted_iota(jnp.int32, (2 * rows, 1), 0)
        key_valid = valid(place)
        m_s, s_pow, l_s = powers(m, 0, q_source, key_valid, s_buf)
        m_e, e_pow, l_e = powers(m, 1, q_edit, key_valid, e_buf)
        sq = jnp.sum(e_pow * e_pow, axis=0, keepdims=True)
        cr = jnp.sum(e_pow * s_pow, axis=0, keepdims=True)
        new = (m_e, l_e, m_s, l_s, sq, cr)
        return new if stats is None else merge(stats, new)

    key_arrival(member, other).wait_recv()
    stats = score_chunk(member, None)

    def far_chunk(d, stats):
        m = shifted(members - 1 - d)
        key_arrival(m, core).wait_recv()
        key_arrival(m, other).wait_recv()
        return score_chunk(m, stats)

    stats = each(members - 1, far_chunk, stats)

    for i, value in enumerate(stats):
        st_send[i:i + 1] = value
    for i in (6, 7):
        st_send[i:i + 1] = jnp.zeros((1, width), F32)
    stat_copy = pltpu.make_async_remote_copy(
        src_ref=st_send, dst_ref=st_recv, send_sem=st_sems.at[0], recv_sem=st_sems.at[1],
        device_id=dev(1 - group, member, core),
    )
    stat_copy.start()
    stat_copy.wait_recv()
    m_e, l_e, m_s, l_s, sq, cr = merge(stats, tuple(st_recv[i:i + 1] for i in range(6)))
    inv_e, inv_s = 1.0 / l_e, 1.0 / l_s
    delta = row_weight * (sq * inv_e * inv_e - cr * inv_e * inv_s)

    def kg_copy(m, c):
        return pltpu.make_async_remote_copy(
            src_ref=kg_send.at[m, c], dst_ref=kg_recv.at[member, core],
            send_sem=kgsend_sem.at[m, c], recv_sem=kgrecv_sem.at[member, core],
            device_id=dev(group, m, c),
        )

    def kg_arrival(m, c):
        return pltpu.make_async_remote_copy(
            src_ref=kg_send.at[m, c], dst_ref=kg_recv.at[m, c],
            send_sem=kgsend_sem.at[m, c], recv_sem=kgrecv_sem.at[m, c],
            device_id=dev(group, m, c),
        )

    def qg_copy(g, c):
        return pltpu.make_async_remote_copy(
            src_ref=qg_send.at[g, c], dst_ref=qg_recv.at[group, core],
            send_sem=qgsend_sem.at[g, c], recv_sem=qgrecv_sem.at[group, core],
            device_id=dev(g, member, c),
        )

    def qg_arrival(g, c):
        return pltpu.make_async_remote_copy(
            src_ref=qg_send.at[g, c], dst_ref=qg_recv.at[g, c],
            send_sem=qgsend_sem.at[g, c], recv_sem=qgrecv_sem.at[g, c],
            device_id=dev(g, member, c),
        )

    def grad_chunk(m, q_total):
        prob_e = e_buf[m] * (jnp.exp(m_buf[m, 1:2] - m_e) * inv_e)
        prob_s = s_buf[m] * (jnp.exp(m_buf[m, 0:1] - m_s) * inv_s)
        grad = (prob_e * (row_weight * (prob_e - prob_s) - delta)).astype(BF16)
        k_part = jnp.dot(grad, q_edit, preferred_element_type=F32) * scale
        q_part = lax.dot_general(
            keys(m, 1), grad, (((0,), (0,)), ((), ())), preferred_element_type=F32
        )
        return k_part, q_part if q_total is None else q_total + q_part

    def far_grad(d, q_total):
        m = shifted(members - 1 - d)
        k_part, q_total = grad_chunk(m, q_total)
        for c in (0, 1):
            kg_send[m, c] = k_part[c * rows:(c + 1) * rows].astype(BF16)
            kg_copy(m, c).start()
        return q_total

    q_total = each(members - 1, far_grad, jnp.zeros((HEAD_DIM, width), F32))
    k_part, q_total = grad_chunk(member, q_total)
    for c in (0, 1):
        kg_own[c] = k_part[c * rows:(c + 1) * rows]
    kg_send[member, other] = kg_own[other].astype(BF16)
    kg_copy(member, other).start()

    q_rows = q_total.T * scale
    for g in (0, 1):
        for c in (0, 1):
            part = q_rows[(2 * g + c) * rows:(2 * g + c + 1) * rows]
            qg_own[g, c] = part
            qg_send[g, c] = part.astype(BF16)
    qg_copy(1 - group, core).start()
    qg_copy(1 - group, other).start()
    qg_copy(group, other).start()

    def put(ref, mine, theirs):
        ref[:, :HEAD_DIM] = jnp.where(core == 0, mine, theirs)
        ref[:, HEAD_DIM:] = jnp.where(core == 0, theirs, mine)

    kg_arrival(member, other).wait_recv()

    def add_far(d, sums):
        mine, theirs = sums
        m = shifted(d + 1)
        kg_arrival(m, core).wait_recv()
        kg_arrival(m, other).wait_recv()
        return mine + kg_recv[m, core].astype(F32), theirs + kg_recv[m, other].astype(F32)

    sums = each(members - 1, add_far, (kg_own[core], kg_recv[member, other].astype(F32)))
    put(kg_ref, *sums)

    qg_arrival(group, other).wait_recv()
    qg_arrival(1 - group, core).wait_recv()
    qg_arrival(1 - group, other).wait_recv()
    put(
        qg_ref,
        qg_own[group, core] + qg_recv[1 - group, core].astype(F32),
        qg_recv[group, other].astype(F32) + qg_recv[1 - group, other].astype(F32),
    )

    def drain(d, carry):
        m = shifted(d + 1)
        for c in (0, 1):
            key_copy(m, c, False).wait_send()
            kg_copy(m, c).wait_send()
        return carry

    each(members - 1, drain, 0)
    key_copy(member, other, False).wait_send()
    kg_copy(member, other).wait_send()
    for copy in (query_copy(1 - group, core, True), query_copy(1 - group, other, False),
                 query_copy(group, other, False), qg_copy(1 - group, core),
                 qg_copy(1 - group, other), qg_copy(group, other), stat_copy):
        copy.wait_send()


def solution(mesh):
    chips = mesh.shape["ctx"] // 2
    members = chips // 2

    def local(query_source, key_source, query_edit, key_edit, text_count):
        rows, full = query_source.shape
        width = 4 * rows
        dma = pltpu.SemaphoreType.DMA
        vmem = pltpu.VMEM
        any_spec = pl.BlockSpec(memory_space=pl.ANY)
        return pl.pallas_call(
            functools.partial(kernel, chips),
            out_shape=(
                jax.ShapeDtypeStruct((rows, full), F32),
                jax.ShapeDtypeStruct((rows, full), F32),
            ),
            in_specs=[pl.BlockSpec(memory_space=pltpu.SMEM)] + [any_spec] * 4,
            out_specs=(pl.BlockSpec(memory_space=pltpu.VMEM),) * 2,
            scratch_shapes=[
                vmem((members, 2, 2, rows, HEAD_DIM), BF16),
                vmem((2, rows, HEAD_DIM), BF16),
                vmem((2, 2, 2, rows, HEAD_DIM), BF16),
                vmem((2, rows, HEAD_DIM), BF16),
                vmem((members, 2 * rows, width), F32),
                vmem((members, 2 * rows, width), F32),
                vmem((members, 8, width), F32),
                vmem((8, width), F32),
                vmem((8, width), F32),
                vmem((members, 2, rows, HEAD_DIM), BF16),
                vmem((members, 2, rows, HEAD_DIM), BF16),
                vmem((2, 2, rows, HEAD_DIM), BF16),
                vmem((2, 2, rows, HEAD_DIM), BF16),
                vmem((2, rows, HEAD_DIM), F32),
                vmem((2, 2, rows, HEAD_DIM), F32),
                dma((8,)),
                dma((members, 2)),
                dma((members, 2)),
                dma((2, 2)),
                dma((2, 2)),
                dma((2,)),
                dma((members, 2)),
                dma((members, 2)),
                dma((2, 2)),
                dma((2, 2)),
            ],
            compiler_params=pltpu.CompilerParams(collective_id=0, has_side_effects=True),
        )(text_count, query_source, key_source, query_edit, key_edit)

    spec = P(("req", "ctx"), None)
    return jax.shard_map(
        local, mesh=mesh, in_specs=(spec,) * 4 + (P("req"),), out_specs=(spec, spec), check_vma=False
    )
```

```python
import functools
import math

import jax
import jax.numpy as jnp
from jax import lax
from jax.experimental import pallas as pl
from jax.experimental.pallas import tpu as pltpu
from jax.sharding import PartitionSpec as P

HEAD_DIM = 128
MASKED = -1e30
SQUARE = True
F32 = jnp.float32
BF16 = jnp.bfloat16


def kernel(
    chips,
    count_ref, qs_hbm, ks_hbm, qe_hbm, ke_hbm,
    qg_ref, kg_ref,
    krecv, kother, qrecv, qother, e_buf, s_buf, m_buf, st_send, st_recv,
    kg_send, kg_recv, qg_send, qg_recv, kg_own, qg_own,
    load_sem, ksend_sem, krecv_sem, qsend_sem, qrecv_sem, st_sems,
    kgsend_sem, kgrecv_sem, qgsend_sem, qgrecv_sem,
):
    members = chips // 2
    rows = krecv.shape[3]
    all_rows = rows * chips * 2
    text_slots = min(512, all_rows // 4)
    scale = 1.0 / math.sqrt(HEAD_DIM)
    weight = 4.0 * all_rows * math.sqrt(all_rows)
    me = lax.axis_index("ctx")
    chip, core = me // 2, me % 2
    other = 1 - core

    if SQUARE:
        group, member = chip // members, chip % members
        chip_of = lambda g, m: g * members + m
    else:
        group, member = chip % 2, chip // 2
        chip_of = lambda g, m: m * 2 + g

    def dev(g, m, c):
        return {"ctx": chip_of(g, m) * 2 + c}

    def shifted(d):
        return (member + d) % members

    def each(n, body, init):
        if n <= 8:
            for i in range(n):
                init = body(i, init)
            return init
        return lax.fori_loop(0, n, body, init)

    own_cols = pl.ds(pl.multiple_of(core * HEAD_DIM, HEAD_DIM), HEAD_DIM)
    other_cols = pl.ds(pl.multiple_of(other * HEAD_DIM, HEAD_DIM), HEAD_DIM)
    loads = []
    for i, (src, dst_own, dst_other) in enumerate((
        (ks_hbm, krecv.at[member, core, 0], kother.at[0]),
        (ke_hbm, krecv.at[member, core, 1], kother.at[1]),
        (qs_hbm, qrecv.at[group, core, 0], qother.at[0]),
        (qe_hbm, qrecv.at[group, core, 1], qother.at[1]),
    )):
        loads.append(pltpu.make_async_copy(src.at[:, own_cols], dst_own, load_sem.at[2 * i]))
        loads.append(pltpu.make_async_copy(src.at[:, other_cols], dst_other, load_sem.at[2 * i + 1]))
    for load in loads:
        load.start()

    barrier = pltpu.get_barrier_semaphore()

    def greet(d, carry):
        for c in (0, 1):
            pl.semaphore_signal(barrier, inc=1, device_id=dev(group, shifted(d + 1), c))
        return carry

    for c in (0, 1):
        pl.semaphore_signal(barrier, inc=1, device_id=dev(1 - group, member, c))
    pl.semaphore_signal(barrier, inc=1, device_id=dev(group, member, other))
    each(members - 1, greet, 0)
    pl.semaphore_wait(barrier, 2 * members + 1)
    for load in loads:
        load.wait()

    def key_copy(m, c, same):
        return pltpu.make_async_remote_copy(
            src_ref=krecv.at[member, core] if same else kother,
            dst_ref=krecv.at[member, core],
            send_sem=ksend_sem.at[m, c],
            recv_sem=krecv_sem.at[member, core],
            device_id=dev(group, m, c),
        )

    def key_arrival(m, c):
        return pltpu.make_async_remote_copy(
            src_ref=kother,
            dst_ref=krecv.at[m, c],
            send_sem=ksend_sem.at[m, c],
            recv_sem=krecv_sem.at[m, c],
            device_id=dev(group, m, c),
        )

    def query_copy(g, c, same):
        return pltpu.make_async_remote_copy(
            src_ref=qrecv.at[group, core] if same else qother,
            dst_ref=qrecv.at[group, core],
            send_sem=qsend_sem.at[g, c],
            recv_sem=qrecv_sem.at[group, core],
            device_id=dev(g, member, c),
        )

    def query_arrival(g, c):
        return pltpu.make_async_remote_copy(
            src_ref=qother,
            dst_ref=qrecv.at[g, c],
            send_sem=qsend_sem.at[g, c],
            recv_sem=qrecv_sem.at[g, c],
            device_id=dev(g, member, c),
        )

    query_copy(1 - group, core, True).start()
    query_copy(1 - group, other, False).start()
    query_copy(group, other, False).start()
    key_copy(member, other, False).start()

    def send_keys(d, carry):
        m = shifted(d + 1)
        key_copy(m, core, True).start()
        key_copy(m, other, False).start()
        return carry

    each(members - 1, send_keys, 0)

    count = count_ref[0]

    def valid(positions):
        return (positions >= text_slots) | (positions < count)

    query_arrival(group, other).wait_recv()
    query_arrival(1 - group, core).wait_recv()
    query_arrival(1 - group, other).wait_recv()

    def queries(which):
        pieces = [qrecv[g, c, which].astype(F32) for g in (0, 1) for c in (0, 1)]
        return jnp.concatenate(pieces, axis=0).astype(BF16)

    q_source, q_edit = queries(0), queries(1)
    width = 4 * rows
    lane = lax.broadcasted_iota(jnp.int32, (1, width), 1)
    piece = lane // rows
    lane_chip = jnp.where(piece < 2, chip_of(0, member), chip_of(1, member))
    row_place = (lane_chip * 2 + piece % 2) * rows + lane % rows
    row_weight = jnp.where(valid(row_place), 2.0 * weight, 0.0)

    def keys(m, which):
        pieces = [krecv[m, c, which].astype(F32) for c in (0, 1)]
        return jnp.concatenate(pieces, axis=0).astype(BF16)

    def merge(a, b):
        me1, le1, ms1, ls1, sq1, cr1 = a
        me2, le2, ms2, ls2, sq2, cr2 = b
        m_e, m_s = jnp.maximum(me1, me2), jnp.maximum(ms1, ms2)
        fe1, fe2 = jnp.exp(me1 - m_e), jnp.exp(me2 - m_e)
        fs1, fs2 = jnp.exp(ms1 - m_s), jnp.exp(ms2 - m_s)
        return (
            m_e, le1 * fe1 + le2 * fe2,
            m_s, ls1 * fs1 + ls2 * fs2,
            sq1 * fe1 * fe1 + sq2 * fe2 * fe2,
            cr1 * fe1 * fs1 + cr2 * fe2 * fs2,
        )

    def powers(m, which, q, key_valid, buf):
        scores = lax.dot_general(
            keys(m, which), q, (((1,), (1,)), ((), ())), preferred_element_type=F32
        ) * scale
        scores = jnp.where(key_valid, scores, MASKED)
        top = jnp.max(scores, axis=0, keepdims=True)
        power = jnp.where(key_valid, jnp.exp(scores - top), 0.0)
        buf[m] = power
        m_buf[m, which:which + 1] = top
        return top, power, jnp.sum(power, axis=0, keepdims=True)

    def score_chunk(m, stats):
        place = chip_of(group, m) * (2 * rows) + lax.broadcasted_iota(jnp.int32, (2 * rows, 1), 0)
        key_valid = valid(place)
        m_s, s_pow, l_s = powers(m, 0, q_source, key_valid, s_buf)
        m_e, e_pow, l_e = powers(m, 1, q_edit, key_valid, e_buf)
        sq = jnp.sum(e_pow * e_pow, axis=0, keepdims=True)
        cr = jnp.sum(e_pow * s_pow, axis=0, keepdims=True)
        new = (m_e, l_e, m_s, l_s, sq, cr)
        return new if stats is None else merge(stats, new)

    key_arrival(member, other).wait_recv()
    stats = score_chunk(member, None)

    def far_chunk(d, stats):
        m = shifted(members - 1 - d)
        key_arrival(m, core).wait_recv()
        key_arrival(m, other).wait_recv()
        return score_chunk(m, stats)

    stats = each(members - 1, far_chunk, stats)

    for i, value in enumerate(stats):
        st_send[i:i + 1] = value
    for i in (6, 7):
        st_send[i:i + 1] = jnp.zeros((1, width), F32)
    stat_copy = pltpu.make_async_remote_copy(
        src_ref=st_send, dst_ref=st_recv, send_sem=st_sems.at[0], recv_sem=st_sems.at[1],
        device_id=dev(1 - group, member, core),
    )
    stat_copy.start()
    stat_copy.wait_recv()
    m_e, l_e, m_s, l_s, sq, cr = merge(stats, tuple(st_recv[i:i + 1] for i in range(6)))
    inv_e, inv_s = 1.0 / l_e, 1.0 / l_s
    delta = row_weight * (sq * inv_e * inv_e - cr * inv_e * inv_s)

    def kg_copy(m, c):
        return pltpu.make_async_remote_copy(
            src_ref=kg_send.at[m, c], dst_ref=kg_recv.at[member, core],
            send_sem=kgsend_sem.at[m, c], recv_sem=kgrecv_sem.at[member, core],
            device_id=dev(group, m, c),
        )

    def kg_arrival(m, c):
        return pltpu.make_async_remote_copy(
            src_ref=kg_send.at[m, c], dst_ref=kg_recv.at[m, c],
            send_sem=kgsend_sem.at[m, c], recv_sem=kgrecv_sem.at[m, c],
            device_id=dev(group, m, c),
        )

    def qg_copy(g, c):
        return pltpu.make_async_remote_copy(
            src_ref=qg_send.at[g, c], dst_ref=qg_recv.at[group, core],
            send_sem=qgsend_sem.at[g, c], recv_sem=qgrecv_sem.at[group, core],
            device_id=dev(g, member, c),
        )

    def qg_arrival(g, c):
        return pltpu.make_async_remote_copy(
            src_ref=qg_send.at[g, c], dst_ref=qg_recv.at[g, c],
            send_sem=qgsend_sem.at[g, c], recv_sem=qgrecv_sem.at[g, c],
            device_id=dev(g, member, c),
        )

    def grad_chunk(m, q_total):
        prob_e = e_buf[m] * (jnp.exp(m_buf[m, 1:2] - m_e) * inv_e)
        prob_s = s_buf[m] * (jnp.exp(m_buf[m, 0:1] - m_s) * inv_s)
        grad = (prob_e * (row_weight * (prob_e - prob_s) - delta)).astype(BF16)
        k_part = jnp.dot(grad, q_edit, preferred_element_type=F32) * scale
        q_part = lax.dot_general(
            keys(m, 1), grad, (((0,), (0,)), ((), ())), preferred_element_type=F32
        )
        return k_part, q_part if q_total is None else q_total + q_part

    def far_grad(d, q_total):
        m = shifted(members - 1 - d)
        k_part, q_total = grad_chunk(m, q_total)
        for c in (0, 1):
            kg_send[m, c] = k_part[c * rows:(c + 1) * rows].astype(BF16)
            kg_copy(m, c).start()
        return q_total

    q_total = each(members - 1, far_grad, jnp.zeros((HEAD_DIM, width), F32))
    k_part, q_total = grad_chunk(member, q_total)
    for c in (0, 1):
        kg_own[c] = k_part[c * rows:(c + 1) * rows]
    kg_send[member, other] = kg_own[other].astype(BF16)
    kg_copy(member, other).start()

    q_rows = q_total.T * scale
    for g in (0, 1):
        for c in (0, 1):
            part = q_rows[(2 * g + c) * rows:(2 * g + c + 1) * rows]
            qg_own[g, c] = part
            qg_send[g, c] = part.astype(BF16)
    qg_copy(1 - group, core).start()
    qg_copy(1 - group, other).start()
    qg_copy(group, other).start()

    def put(ref, mine, theirs):
        ref[:, :HEAD_DIM] = jnp.where(core == 0, mine, theirs)
        ref[:, HEAD_DIM:] = jnp.where(core == 0, theirs, mine)

    kg_arrival(member, other).wait_recv()

    def add_far(d, sums):
        mine, theirs = sums
        m = shifted(d + 1)
        kg_arrival(m, core).wait_recv()
        kg_arrival(m, other).wait_recv()
        return mine + kg_recv[m, core].astype(F32), theirs + kg_recv[m, other].astype(F32)

    sums = each(members - 1, add_far, (kg_own[core], kg_recv[member, other].astype(F32)))
    put(kg_ref, *sums)

    qg_arrival(group, other).wait_recv()
    qg_arrival(1 - group, core).wait_recv()
    qg_arrival(1 - group, other).wait_recv()
    put(
        qg_ref,
        qg_own[group, core] + qg_recv[1 - group, core].astype(F32),
        qg_recv[group, other].astype(F32) + qg_recv[1 - group, other].astype(F32),
    )

    def drain(d, carry):
        m = shifted(d + 1)
        for c in (0, 1):
            key_copy(m, c, False).wait_send()
            kg_copy(m, c).wait_send()
        return carry

    each(members - 1, drain, 0)
    key_copy(member, other, False).wait_send()
    kg_copy(member, other).wait_send()
    for copy in (query_copy(1 - group, core, True), query_copy(1 - group, other, False),
                 query_copy(group, other, False), qg_copy(1 - group, core),
                 qg_copy(1 - group, other), qg_copy(group, other), stat_copy):
        copy.wait_send()


def solution(mesh):
    chips = mesh.shape["ctx"] // 2
    members = chips // 2

    def local(query_source, key_source, query_edit, key_edit, text_count):
        rows, full = query_source.shape
        width = 4 * rows
        dma = pltpu.SemaphoreType.DMA
        vmem = pltpu.VMEM
        any_spec = pl.BlockSpec(memory_space=pl.ANY)
        return pl.pallas_call(
            functools.partial(kernel, chips),
            out_shape=(
                jax.ShapeDtypeStruct((rows, full), F32),
                jax.ShapeDtypeStruct((rows, full), F32),
            ),
            in_specs=[pl.BlockSpec(memory_space=pltpu.SMEM)] + [any_spec] * 4,
            out_specs=(pl.BlockSpec(memory_space=pltpu.VMEM),) * 2,
            scratch_shapes=[
                vmem((members, 2, 2, rows, HEAD_DIM), BF16),
                vmem((2, rows, HEAD_DIM), BF16),
                vmem((2, 2, 2, rows, HEAD_DIM), BF16),
                vmem((2, rows, HEAD_DIM), BF16),
                vmem((members, 2 * rows, width), F32),
                vmem((members, 2 * rows, width), F32),
                vmem((members, 8, width), F32),
                vmem((8, width), F32),
                vmem((8, width), F32),
                vmem((members, 2, rows, HEAD_DIM), BF16),
                vmem((members, 2, rows, HEAD_DIM), BF16),
                vmem((2, 2, rows, HEAD_DIM), BF16),
                vmem((2, 2, rows, HEAD_DIM), BF16),
                vmem((2, rows, HEAD_DIM), F32),
                vmem((2, 2, rows, HEAD_DIM), F32),
                dma((8,)),
                dma((members, 2)),
                dma((members, 2)),
                dma((2, 2)),
                dma((2, 2)),
                dma((2,)),
                dma((members, 2)),
                dma((members, 2)),
                dma((2, 2)),
                dma((2, 2)),
            ],
            compiler_params=pltpu.CompilerParams(collective_id=0, has_side_effects=True),
        )(text_count, query_source, key_source, query_edit, key_edit)

    spec = P(("req", "ctx"), None)
    return jax.shard_map(
        local, mesh=mesh, in_specs=(spec,) * 4 + (P("req"),), out_specs=(spec, spec), check_vma=False
    )
```

```python
import functools
import math

import jax
import jax.numpy as jnp
from jax import lax
from jax.experimental import pallas as pl
from jax.experimental.pallas import tpu as pltpu
from jax.sharding import PartitionSpec as P

HEAD_DIM = 128
MASKED = -1e30
SQUARE = True
F32 = jnp.float32
BF16 = jnp.bfloat16


def kernel(
    chips,
    count_hbm, qs_hbm, ks_hbm, qe_hbm, ke_hbm,
    qg_ref, kg_ref,
    count_ref, krecv, kother, qrecv, qother, e_buf, s_buf, m_buf, st_send, st_recv,
    kg_send, kg_recv, qg_send, qg_recv, kg_own, qg_own,
    load_sem, ksend_sem, krecv_sem, qsend_sem, qrecv_sem, st_sems,
    kgsend_sem, kgrecv_sem, qgsend_sem, qgrecv_sem,
):
    members = chips // 2
    rows = krecv.shape[3]
    all_rows = rows * chips * 2
    text_slots = min(512, all_rows // 4)
    scale = 1.0 / math.sqrt(HEAD_DIM)
    weight = 4.0 * all_rows * math.sqrt(all_rows)
    me = lax.axis_index("ctx")
    chip, core = me // 2, me % 2
    other = 1 - core

    if SQUARE:
        group, member = chip // members, chip % members
        chip_of = lambda g, m: g * members + m
    else:
        group, member = chip % 2, chip // 2
        chip_of = lambda g, m: m * 2 + g

    def dev(g, m, c):
        return {"ctx": chip_of(g, m) * 2 + c}

    def shifted(d):
        return (member + d) % members

    def each(n, body, init):
        if n <= 8:
            for i in range(n):
                init = body(i, init)
            return init
        return lax.fori_loop(0, n, body, init)

    own_cols = pl.ds(pl.multiple_of(core * HEAD_DIM, HEAD_DIM), HEAD_DIM)
    other_cols = pl.ds(pl.multiple_of(other * HEAD_DIM, HEAD_DIM), HEAD_DIM)
    loads = []
    for i, (src, dst_own, dst_other) in enumerate((
        (ks_hbm, krecv.at[member, core, 0], kother.at[0]),
        (ke_hbm, krecv.at[member, core, 1], kother.at[1]),
        (qs_hbm, qrecv.at[group, core, 0], qother.at[0]),
        (qe_hbm, qrecv.at[group, core, 1], qother.at[1]),
    )):
        loads.append(pltpu.make_async_copy(src.at[:, own_cols], dst_own, load_sem.at[2 * i]))
        loads.append(pltpu.make_async_copy(src.at[:, other_cols], dst_other, load_sem.at[2 * i + 1]))
    loads.append(pltpu.make_async_copy(count_hbm, count_ref, load_sem.at[8]))
    for load in loads:
        load.start()

    barrier = pltpu.get_barrier_semaphore()

    def greet(d, carry):
        for c in (0, 1):
            pl.semaphore_signal(barrier, inc=1, device_id=dev(group, shifted(d + 1), c))
        return carry

    for c in (0, 1):
        pl.semaphore_signal(barrier, inc=1, device_id=dev(1 - group, member, c))
    pl.semaphore_signal(barrier, inc=1, device_id=dev(group, member, other))
    each(members - 1, greet, 0)
    pl.semaphore_wait(barrier, 2 * members + 1)
    for load in loads:
        load.wait()

    def key_copy(m, c, same):
        return pltpu.make_async_remote_copy(
            src_ref=krecv.at[member, core] if same else kother,
            dst_ref=krecv.at[member, core],
            send_sem=ksend_sem.at[m, c],
            recv_sem=krecv_sem.at[member, core],
            device_id=dev(group, m, c),
        )

    def key_arrival(m, c):
        return pltpu.make_async_remote_copy(
            src_ref=kother,
            dst_ref=krecv.at[m, c],
            send_sem=ksend_sem.at[m, c],
            recv_sem=krecv_sem.at[m, c],
            device_id=dev(group, m, c),
        )

    def query_copy(g, c, same):
        return pltpu.make_async_remote_copy(
            src_ref=qrecv.at[group, core] if same else qother,
            dst_ref=qrecv.at[group, core],
            send_sem=qsend_sem.at[g, c],
            recv_sem=qrecv_sem.at[group, core],
            device_id=dev(g, member, c),
        )

    def query_arrival(g, c):
        return pltpu.make_async_remote_copy(
            src_ref=qother,
            dst_ref=qrecv.at[g, c],
            send_sem=qsend_sem.at[g, c],
            recv_sem=qrecv_sem.at[g, c],
            device_id=dev(g, member, c),
        )

    query_copy(1 - group, core, True).start()
    query_copy(1 - group, other, False).start()
    query_copy(group, other, False).start()
    key_copy(member, other, False).start()

    def send_keys(d, carry):
        m = shifted(d + 1)
        key_copy(m, core, True).start()
        key_copy(m, other, False).start()
        return carry

    each(members - 1, send_keys, 0)

    count = count_ref[0]

    def valid(positions):
        return (positions >= text_slots) | (positions < count)

    query_arrival(group, other).wait_recv()
    query_arrival(1 - group, core).wait_recv()
    query_arrival(1 - group, other).wait_recv()

    def queries(which):
        pieces = [qrecv[g, c, which].astype(F32) for g in (0, 1) for c in (0, 1)]
        return jnp.concatenate(pieces, axis=0).astype(BF16)

    q_source, q_edit = queries(0), queries(1)
    width = 4 * rows
    lane = lax.broadcasted_iota(jnp.int32, (1, width), 1)
    piece = lane // rows
    lane_chip = jnp.where(piece < 2, chip_of(0, member), chip_of(1, member))
    row_place = (lane_chip * 2 + piece % 2) * rows + lane % rows
    row_weight = jnp.where(valid(row_place), 2.0 * weight, 0.0)

    def keys(m, which):
        pieces = [krecv[m, c, which].astype(F32) for c in (0, 1)]
        return jnp.concatenate(pieces, axis=0).astype(BF16)

    def merge(a, b):
        me1, le1, ms1, ls1, sq1, cr1 = a
        me2, le2, ms2, ls2, sq2, cr2 = b
        m_e, m_s = jnp.maximum(me1, me2), jnp.maximum(ms1, ms2)
        fe1, fe2 = jnp.exp(me1 - m_e), jnp.exp(me2 - m_e)
        fs1, fs2 = jnp.exp(ms1 - m_s), jnp.exp(ms2 - m_s)
        return (
            m_e, le1 * fe1 + le2 * fe2,
            m_s, ls1 * fs1 + ls2 * fs2,
            sq1 * fe1 * fe1 + sq2 * fe2 * fe2,
            cr1 * fe1 * fs1 + cr2 * fe2 * fs2,
        )

    def powers(m, which, q, key_valid, buf):
        scores = lax.dot_general(
            keys(m, which), q, (((1,), (1,)), ((), ())), preferred_element_type=F32
        ) * scale
        scores = jnp.where(key_valid, scores, MASKED)
        top = jnp.max(scores, axis=0, keepdims=True)
        power = jnp.where(key_valid, jnp.exp(scores - top), 0.0)
        buf[m] = power
        m_buf[m, which:which + 1] = top
        return top, power, jnp.sum(power, axis=0, keepdims=True)

    def score_chunk(m, stats):
        place = chip_of(group, m) * (2 * rows) + lax.broadcasted_iota(jnp.int32, (2 * rows, 1), 0)
        key_valid = valid(place)
        m_s, s_pow, l_s = powers(m, 0, q_source, key_valid, s_buf)
        m_e, e_pow, l_e = powers(m, 1, q_edit, key_valid, e_buf)
        sq = jnp.sum(e_pow * e_pow, axis=0, keepdims=True)
        cr = jnp.sum(e_pow * s_pow, axis=0, keepdims=True)
        new = (m_e, l_e, m_s, l_s, sq, cr)
        return new if stats is None else merge(stats, new)

    key_arrival(member, other).wait_recv()
    stats = score_chunk(member, None)

    def far_chunk(d, stats):
        m = shifted(members - 1 - d)
        key_arrival(m, core).wait_recv()
        key_arrival(m, other).wait_recv()
        return score_chunk(m, stats)

    stats = each(members - 1, far_chunk, stats)

    for i, value in enumerate(stats):
        st_send[i:i + 1] = value
    for i in (6, 7):
        st_send[i:i + 1] = jnp.zeros((1, width), F32)
    stat_copy = pltpu.make_async_remote_copy(
        src_ref=st_send, dst_ref=st_recv, send_sem=st_sems.at[0], recv_sem=st_sems.at[1],
        device_id=dev(1 - group, member, core),
    )
    stat_copy.start()
    stat_copy.wait_recv()
    m_e, l_e, m_s, l_s, sq, cr = merge(stats, tuple(st_recv[i:i + 1] for i in range(6)))
    inv_e, inv_s = 1.0 / l_e, 1.0 / l_s
    delta = row_weight * (sq * inv_e * inv_e - cr * inv_e * inv_s)

    def kg_copy(m, c):
        return pltpu.make_async_remote_copy(
            src_ref=kg_send.at[m, c], dst_ref=kg_recv.at[member, core],
            send_sem=kgsend_sem.at[m, c], recv_sem=kgrecv_sem.at[member, core],
            device_id=dev(group, m, c),
        )

    def kg_arrival(m, c):
        return pltpu.make_async_remote_copy(
            src_ref=kg_send.at[m, c], dst_ref=kg_recv.at[m, c],
            send_sem=kgsend_sem.at[m, c], recv_sem=kgrecv_sem.at[m, c],
            device_id=dev(group, m, c),
        )

    def qg_copy(g, c):
        return pltpu.make_async_remote_copy(
            src_ref=qg_send.at[g, c], dst_ref=qg_recv.at[group, core],
            send_sem=qgsend_sem.at[g, c], recv_sem=qgrecv_sem.at[group, core],
            device_id=dev(g, member, c),
        )

    def qg_arrival(g, c):
        return pltpu.make_async_remote_copy(
            src_ref=qg_send.at[g, c], dst_ref=qg_recv.at[g, c],
            send_sem=qgsend_sem.at[g, c], recv_sem=qgrecv_sem.at[g, c],
            device_id=dev(g, member, c),
        )

    def grad_chunk(m, q_total):
        prob_e = e_buf[m] * (jnp.exp(m_buf[m, 1:2] - m_e) * inv_e)
        prob_s = s_buf[m] * (jnp.exp(m_buf[m, 0:1] - m_s) * inv_s)
        grad = (prob_e * (row_weight * (prob_e - prob_s) - delta)).astype(BF16)
        k_part = jnp.dot(grad, q_edit, preferred_element_type=F32) * scale
        q_part = lax.dot_general(
            keys(m, 1), grad, (((0,), (0,)), ((), ())), preferred_element_type=F32
        )
        return k_part, q_part if q_total is None else q_total + q_part

    def far_grad(d, q_total):
        m = shifted(members - 1 - d)
        k_part, q_total = grad_chunk(m, q_total)
        for c in (0, 1):
            kg_send[m, c] = k_part[c * rows:(c + 1) * rows].astype(BF16)
            kg_copy(m, c).start()
        return q_total

    q_total = each(members - 1, far_grad, jnp.zeros((HEAD_DIM, width), F32))
    k_part, q_total = grad_chunk(member, q_total)
    for c in (0, 1):
        kg_own[c] = k_part[c * rows:(c + 1) * rows]
    kg_send[member, other] = kg_own[other].astype(BF16)
    kg_copy(member, other).start()

    q_rows = q_total.T * scale
    for g in (0, 1):
        for c in (0, 1):
            part = q_rows[(2 * g + c) * rows:(2 * g + c + 1) * rows]
            qg_own[g, c] = part
            qg_send[g, c] = part.astype(BF16)
    qg_copy(1 - group, core).start()
    qg_copy(1 - group, other).start()
    qg_copy(group, other).start()

    def put(ref, mine, theirs):
        ref[:, :HEAD_DIM] = jnp.where(core == 0, mine, theirs)
        ref[:, HEAD_DIM:] = jnp.where(core == 0, theirs, mine)

    kg_arrival(member, other).wait_recv()

    def add_far(d, sums):
        mine, theirs = sums
        m = shifted(d + 1)
        kg_arrival(m, core).wait_recv()
        kg_arrival(m, other).wait_recv()
        return mine + kg_recv[m, core].astype(F32), theirs + kg_recv[m, other].astype(F32)

    sums = each(members - 1, add_far, (kg_own[core], kg_recv[member, other].astype(F32)))
    put(kg_ref, *sums)

    qg_arrival(group, other).wait_recv()
    qg_arrival(1 - group, core).wait_recv()
    qg_arrival(1 - group, other).wait_recv()
    put(
        qg_ref,
        qg_own[group, core] + qg_recv[1 - group, core].astype(F32),
        qg_recv[group, other].astype(F32) + qg_recv[1 - group, other].astype(F32),
    )

    def drain(d, carry):
        m = shifted(d + 1)
        for c in (0, 1):
            key_copy(m, c, False).wait_send()
            kg_copy(m, c).wait_send()
        return carry

    each(members - 1, drain, 0)
    key_copy(member, other, False).wait_send()
    kg_copy(member, other).wait_send()
    for copy in (query_copy(1 - group, core, True), query_copy(1 - group, other, False),
                 query_copy(group, other, False), qg_copy(1 - group, core),
                 qg_copy(1 - group, other), qg_copy(group, other), stat_copy):
        copy.wait_send()


def solution(mesh):
    chips = mesh.shape["ctx"] // 2
    members = chips // 2

    def local(query_source, key_source, query_edit, key_edit, text_count):
        rows, full = query_source.shape
        width = 4 * rows
        dma = pltpu.SemaphoreType.DMA
        vmem = pltpu.VMEM
        any_spec = pl.BlockSpec(memory_space=pl.ANY)
        return pl.pallas_call(
            functools.partial(kernel, chips),
            out_shape=(
                pltpu.VMEM((rows, full), F32),
                pltpu.VMEM((rows, full), F32),
            ),
            in_specs=[any_spec] * 5,
            out_specs=(pl.BlockSpec(memory_space=pltpu.VMEM),) * 2,
            scratch_shapes=[
                pltpu.SMEM((1,), jnp.int32),
                vmem((members, 2, 2, rows, HEAD_DIM), BF16),
                vmem((2, rows, HEAD_DIM), BF16),
                vmem((2, 2, 2, rows, HEAD_DIM), BF16),
                vmem((2, rows, HEAD_DIM), BF16),
                vmem((members, 2 * rows, width), F32),
                vmem((members, 2 * rows, width), F32),
                vmem((members, 8, width), F32),
                vmem((8, width), F32),
                vmem((8, width), F32),
                vmem((members, 2, rows, HEAD_DIM), BF16),
                vmem((members, 2, rows, HEAD_DIM), BF16),
                vmem((2, 2, rows, HEAD_DIM), BF16),
                vmem((2, 2, rows, HEAD_DIM), BF16),
                vmem((2, rows, HEAD_DIM), F32),
                vmem((2, 2, rows, HEAD_DIM), F32),
                dma((9,)),
                dma((members, 2)),
                dma((members, 2)),
                dma((2, 2)),
                dma((2, 2)),
                dma((2,)),
                dma((members, 2)),
                dma((members, 2)),
                dma((2, 2)),
                dma((2, 2)),
            ],
            compiler_params=pltpu.CompilerParams(collective_id=0, has_side_effects=True),
        )(text_count, query_source, key_source, query_edit, key_edit)

    spec = P(("req", "ctx"), None)
    return jax.shard_map(
        local, mesh=mesh, in_specs=(spec,) * 4 + (P("req"),), out_specs=(spec, spec), check_vma=False
    )
```

```python
import functools
import math

import jax
import jax.numpy as jnp
from jax import lax
from jax.experimental import pallas as pl
from jax.experimental.pallas import tpu as pltpu
from jax.sharding import PartitionSpec as P

HEAD_DIM = 128
MASKED = -1e30
SQUARE = True
F32 = jnp.float32
BF16 = jnp.bfloat16


def kernel(
    chips,
    count_hbm, qs_hbm, ks_hbm, qe_hbm, ke_hbm,
    qg_ref, kg_ref,
    count_ref, krecv, kother, qrecv, qother, e_buf, s_buf, m_buf, st_send, st_recv,
    kg_send, kg_recv, qg_send, qg_recv, kg_own, qg_own,
    load_sem, ksend_sem, krecv_sem, qsend_sem, qrecv_sem, st_sems,
    kgsend_sem, kgrecv_sem, qgsend_sem, qgrecv_sem,
):
    members = chips // 2
    rows = krecv.shape[3]
    all_rows = rows * chips * 2
    text_slots = min(512, all_rows // 4)
    scale = 1.0 / math.sqrt(HEAD_DIM)
    weight = 4.0 * all_rows * math.sqrt(all_rows)
    me = lax.axis_index("ctx")
    chip, core = me // 2, me % 2
    other = 1 - core

    if SQUARE:
        group, member = chip // members, chip % members
        chip_of = lambda g, m: g * members + m
    else:
        group, member = chip % 2, chip // 2
        chip_of = lambda g, m: m * 2 + g

    def dev(g, m, c):
        return {"ctx": chip_of(g, m) * 2 + c}

    def shifted(d):
        return (member + d) % members

    def each(n, body, init):
        if n <= 8:
            for i in range(n):
                init = body(i, init)
            return init
        return lax.fori_loop(0, n, body, init)

    own_cols = pl.ds(pl.multiple_of(core * HEAD_DIM, HEAD_DIM), HEAD_DIM)
    other_cols = pl.ds(pl.multiple_of(other * HEAD_DIM, HEAD_DIM), HEAD_DIM)
    loads = []
    for i, (src, dst_own, dst_other) in enumerate((
        (ks_hbm, krecv.at[member, core, 0], kother.at[0]),
        (ke_hbm, krecv.at[member, core, 1], kother.at[1]),
        (qs_hbm, qrecv.at[group, core, 0], qother.at[0]),
        (qe_hbm, qrecv.at[group, core, 1], qother.at[1]),
    )):
        loads.append(pltpu.make_async_copy(src.at[:, own_cols], dst_own, load_sem.at[2 * i]))
        loads.append(pltpu.make_async_copy(src.at[:, other_cols], dst_other, load_sem.at[2 * i + 1]))
    loads.append(pltpu.make_async_copy(count_hbm, count_ref, load_sem.at[8]))
    for load in loads:
        load.start()

    barrier = pltpu.get_barrier_semaphore()

    def greet(d, carry):
        for c in (0, 1):
            pl.semaphore_signal(barrier, inc=1, device_id=dev(group, shifted(d + 1), c))
        return carry

    for c in (0, 1):
        pl.semaphore_signal(barrier, inc=1, device_id=dev(1 - group, member, c))
    pl.semaphore_signal(barrier, inc=1, device_id=dev(group, member, other))
    each(members - 1, greet, 0)
    pl.semaphore_wait(barrier, 2 * members + 1)
    for load in loads:
        load.wait()

    def key_copy(m, c, same):
        return pltpu.make_async_remote_copy(
            src_ref=krecv.at[member, core] if same else kother,
            dst_ref=krecv.at[member, core],
            send_sem=ksend_sem.at[m, c],
            recv_sem=krecv_sem.at[member, core],
            device_id=dev(group, m, c),
        )

    def key_arrival(m, c):
        return pltpu.make_async_remote_copy(
            src_ref=kother,
            dst_ref=krecv.at[m, c],
            send_sem=ksend_sem.at[m, c],
            recv_sem=krecv_sem.at[m, c],
            device_id=dev(group, m, c),
        )

    def query_copy(g, c, same):
        return pltpu.make_async_remote_copy(
            src_ref=qrecv.at[group, core] if same else qother,
            dst_ref=qrecv.at[group, core],
            send_sem=qsend_sem.at[g, c],
            recv_sem=qrecv_sem.at[group, core],
            device_id=dev(g, member, c),
        )

    def query_arrival(g, c):
        return pltpu.make_async_remote_copy(
            src_ref=qother,
            dst_ref=qrecv.at[g, c],
            send_sem=qsend_sem.at[g, c],
            recv_sem=qrecv_sem.at[g, c],
            device_id=dev(g, member, c),
        )

    query_copy(1 - group, core, True).start()
    query_copy(1 - group, other, False).start()
    query_copy(group, other, False).start()
    key_copy(member, other, False).start()

    def send_keys(d, carry):
        m = shifted(d + 1)
        key_copy(m, core, True).start()
        key_copy(m, other, False).start()
        return carry

    each(members - 1, send_keys, 0)

    count = count_ref[0]

    def valid(positions):
        return (positions >= text_slots) | (positions < count)

    query_arrival(group, other).wait_recv()
    query_arrival(1 - group, core).wait_recv()
    query_arrival(1 - group, other).wait_recv()

    def queries(which):
        pieces = [qrecv[g, c, which].astype(F32) for g in (0, 1) for c in (0, 1)]
        return jnp.concatenate(pieces, axis=0).astype(BF16)

    q_source, q_edit = queries(0), queries(1)
    width = 4 * rows
    lane = lax.broadcasted_iota(jnp.int32, (1, width), 1)
    piece = lane // rows
    lane_chip = jnp.where(piece < 2, chip_of(0, member), chip_of(1, member))
    row_place = (lane_chip * 2 + piece % 2) * rows + lane % rows
    row_weight = jnp.where(valid(row_place), 2.0 * weight, 0.0)

    def keys(m, which):
        pieces = [krecv[m, c, which].astype(F32) for c in (0, 1)]
        return jnp.concatenate(pieces, axis=0).astype(BF16)

    def merge(a, b):
        me1, le1, ms1, ls1, sq1, cr1 = a
        me2, le2, ms2, ls2, sq2, cr2 = b
        m_e, m_s = jnp.maximum(me1, me2), jnp.maximum(ms1, ms2)
        fe1, fe2 = jnp.exp(me1 - m_e), jnp.exp(me2 - m_e)
        fs1, fs2 = jnp.exp(ms1 - m_s), jnp.exp(ms2 - m_s)
        return (
            m_e, le1 * fe1 + le2 * fe2,
            m_s, ls1 * fs1 + ls2 * fs2,
            sq1 * fe1 * fe1 + sq2 * fe2 * fe2,
            cr1 * fe1 * fs1 + cr2 * fe2 * fs2,
        )

    def powers(m, which, q, key_valid, buf):
        scores = lax.dot_general(
            keys(m, which), q, (((1,), (1,)), ((), ())), preferred_element_type=F32
        ) * scale
        scores = jnp.where(key_valid, scores, MASKED)
        top = jnp.max(scores, axis=0, keepdims=True)
        power = jnp.where(key_valid, jnp.exp(scores - top), 0.0)
        buf[m] = power
        m_buf[m, which:which + 1] = top
        return top, power, jnp.sum(power, axis=0, keepdims=True)

    def score_chunk(m, stats):
        place = chip_of(group, m) * (2 * rows) + lax.broadcasted_iota(jnp.int32, (2 * rows, 1), 0)
        key_valid = valid(place)
        m_s, s_pow, l_s = powers(m, 0, q_source, key_valid, s_buf)
        m_e, e_pow, l_e = powers(m, 1, q_edit, key_valid, e_buf)
        sq = jnp.sum(e_pow * e_pow, axis=0, keepdims=True)
        cr = jnp.sum(e_pow * s_pow, axis=0, keepdims=True)
        new = (m_e, l_e, m_s, l_s, sq, cr)
        return new if stats is None else merge(stats, new)

    key_arrival(member, other).wait_recv()
    stats = score_chunk(member, None)

    def far_chunk(d, stats):
        m = shifted(members - 1 - d)
        key_arrival(m, core).wait_recv()
        key_arrival(m, other).wait_recv()
        return score_chunk(m, stats)

    stats = each(members - 1, far_chunk, stats)

    for i, value in enumerate(stats):
        st_send[i:i + 1] = value
    for i in (6, 7):
        st_send[i:i + 1] = jnp.zeros((1, width), F32)
    stat_copy = pltpu.make_async_remote_copy(
        src_ref=st_send, dst_ref=st_recv, send_sem=st_sems.at[0], recv_sem=st_sems.at[1],
        device_id=dev(1 - group, member, core),
    )
    stat_copy.start()
    stat_copy.wait_recv()
    m_e, l_e, m_s, l_s, sq, cr = merge(stats, tuple(st_recv[i:i + 1] for i in range(6)))
    inv_e, inv_s = 1.0 / l_e, 1.0 / l_s
    delta = row_weight * (sq * inv_e * inv_e - cr * inv_e * inv_s)

    def kg_copy(m, c):
        return pltpu.make_async_remote_copy(
            src_ref=kg_send.at[m, c], dst_ref=kg_recv.at[member, core],
            send_sem=kgsend_sem.at[m, c], recv_sem=kgrecv_sem.at[member, core],
            device_id=dev(group, m, c),
        )

    def kg_arrival(m, c):
        return pltpu.make_async_remote_copy(
            src_ref=kg_send.at[m, c], dst_ref=kg_recv.at[m, c],
            send_sem=kgsend_sem.at[m, c], recv_sem=kgrecv_sem.at[m, c],
            device_id=dev(group, m, c),
        )

    def qg_copy(g, c):
        return pltpu.make_async_remote_copy(
            src_ref=qg_send.at[g, c], dst_ref=qg_recv.at[group, core],
            send_sem=qgsend_sem.at[g, c], recv_sem=qgrecv_sem.at[group, core],
            device_id=dev(g, member, c),
        )

    def qg_arrival(g, c):
        return pltpu.make_async_remote_copy(
            src_ref=qg_send.at[g, c], dst_ref=qg_recv.at[g, c],
            send_sem=qgsend_sem.at[g, c], recv_sem=qgrecv_sem.at[g, c],
            device_id=dev(g, member, c),
        )

    def grad_chunk(m, q_total):
        prob_e = e_buf[m] * (jnp.exp(m_buf[m, 1:2] - m_e) * inv_e)
        prob_s = s_buf[m] * (jnp.exp(m_buf[m, 0:1] - m_s) * inv_s)
        grad = (prob_e * (row_weight * (prob_e - prob_s) - delta)).astype(BF16)
        k_part = jnp.dot(grad, q_edit, preferred_element_type=F32) * scale
        q_part = lax.dot_general(
            keys(m, 1), grad, (((0,), (0,)), ((), ())), preferred_element_type=F32
        )
        return k_part, q_part if q_total is None else q_total + q_part

    def far_grad(d, q_total):
        m = shifted(members - 1 - d)
        k_part, q_total = grad_chunk(m, q_total)
        for c in (0, 1):
            kg_send[m, c] = k_part[c * rows:(c + 1) * rows].astype(BF16)
            kg_copy(m, c).start()
        return q_total

    q_total = each(members - 1, far_grad, jnp.zeros((HEAD_DIM, width), F32))
    k_part, q_total = grad_chunk(member, q_total)
    for c in (0, 1):
        kg_own[c] = k_part[c * rows:(c + 1) * rows]
    kg_send[member, other] = kg_own[other].astype(BF16)
    kg_copy(member, other).start()

    q_rows = q_total.T * scale
    for g in (0, 1):
        for c in (0, 1):
            part = q_rows[(2 * g + c) * rows:(2 * g + c + 1) * rows]
            qg_own[g, c] = part
            qg_send[g, c] = part.astype(BF16)
    qg_copy(1 - group, core).start()
    qg_copy(1 - group, other).start()
    qg_copy(group, other).start()

    def put(ref, mine, theirs):
        ref[:, :HEAD_DIM] = jnp.where(core == 0, mine, theirs)
        ref[:, HEAD_DIM:] = jnp.where(core == 0, theirs, mine)

    kg_arrival(member, other).wait_recv()

    def add_far(d, sums):
        mine, theirs = sums
        m = shifted(d + 1)
        kg_arrival(m, core).wait_recv()
        kg_arrival(m, other).wait_recv()
        return mine + kg_recv[m, core].astype(F32), theirs + kg_recv[m, other].astype(F32)

    sums = each(members - 1, add_far, (kg_own[core], kg_recv[member, other].astype(F32)))
    put(kg_ref, *sums)

    qg_arrival(group, other).wait_recv()
    qg_arrival(1 - group, core).wait_recv()
    qg_arrival(1 - group, other).wait_recv()
    put(
        qg_ref,
        qg_own[group, core] + qg_recv[1 - group, core].astype(F32),
        qg_recv[group, other].astype(F32) + qg_recv[1 - group, other].astype(F32),
    )

    def drain(d, carry):
        m = shifted(d + 1)
        for c in (0, 1):
            key_copy(m, c, False).wait_send()
            kg_copy(m, c).wait_send()
        return carry

    each(members - 1, drain, 0)
    key_copy(member, other, False).wait_send()
    kg_copy(member, other).wait_send()
    for copy in (query_copy(1 - group, core, True), query_copy(1 - group, other, False),
                 query_copy(group, other, False), qg_copy(1 - group, core),
                 qg_copy(1 - group, other), qg_copy(group, other), stat_copy):
        copy.wait_send()


def put_out(qg_vmem, kg_vmem, qg_hbm, kg_hbm, sems):
    copies = (
        pltpu.make_async_copy(qg_vmem, qg_hbm, sems.at[0]),
        pltpu.make_async_copy(kg_vmem, kg_hbm, sems.at[1]),
    )
    for copy in copies:
        copy.start()
    for copy in copies:
        copy.wait()


def solution(mesh):
    chips = mesh.shape["ctx"] // 2
    members = chips // 2

    def local(query_source, key_source, query_edit, key_edit, text_count):
        rows, full = query_source.shape
        width = 4 * rows
        dma = pltpu.SemaphoreType.DMA
        vmem = pltpu.VMEM
        any_spec = pl.BlockSpec(memory_space=pl.ANY)
        grads = pl.pallas_call(
            functools.partial(kernel, chips),
            out_shape=(
                pltpu.VMEM((rows, full), F32),
                pltpu.VMEM((rows, full), F32),
            ),
            in_specs=[pl.BlockSpec(memory_space=pltpu.HBM)] * 5,
            out_specs=(pl.BlockSpec(memory_space=pltpu.VMEM),) * 2,
            scratch_shapes=[
                pltpu.SMEM((1,), jnp.int32),
                vmem((members, 2, 2, rows, HEAD_DIM), BF16),
                vmem((2, rows, HEAD_DIM), BF16),
                vmem((2, 2, 2, rows, HEAD_DIM), BF16),
                vmem((2, rows, HEAD_DIM), BF16),
                vmem((members, 2 * rows, width), F32),
                vmem((members, 2 * rows, width), F32),
                vmem((members, 8, width), F32),
                vmem((8, width), F32),
                vmem((8, width), F32),
                vmem((members, 2, rows, HEAD_DIM), BF16),
                vmem((members, 2, rows, HEAD_DIM), BF16),
                vmem((2, 2, rows, HEAD_DIM), BF16),
                vmem((2, 2, rows, HEAD_DIM), BF16),
                vmem((2, rows, HEAD_DIM), F32),
                vmem((2, 2, rows, HEAD_DIM), F32),
                dma((9,)),
                dma((members, 2)),
                dma((members, 2)),
                dma((2, 2)),
                dma((2, 2)),
                dma((2,)),
                dma((members, 2)),
                dma((members, 2)),
                dma((2, 2)),
                dma((2, 2)),
            ],
            compiler_params=pltpu.CompilerParams(collective_id=0, has_side_effects=True),
        )(text_count, query_source, key_source, query_edit, key_edit)
        return pl.pallas_call(
            put_out,
            out_shape=(pltpu.HBM((rows, full), F32),) * 2,
            in_specs=[pl.BlockSpec(memory_space=pltpu.VMEM)] * 2,
            out_specs=(pl.BlockSpec(memory_space=pltpu.HBM),) * 2,
            scratch_shapes=[dma((2,))],
        )(*(pltpu.with_memory_space_constraint(g, pltpu.VMEM) for g in grads))

    spec = P(("req", "ctx"), None)
    return jax.shard_map(
        local, mesh=mesh, in_specs=(spec,) * 4 + (P("req"),), out_specs=(spec, spec), check_vma=False
    )
```

```python
import functools
import math

import jax
import jax.numpy as jnp
from jax import lax
from jax.experimental import pallas as pl
from jax.experimental.pallas import tpu as pltpu
from jax.sharding import PartitionSpec as P

HEAD_DIM = 128
MASKED = -1e30
SQUARE = True
F32 = jnp.float32
BF16 = jnp.bfloat16


def kernel(
    chips,
    count_hbm, qs_hbm, ks_hbm, qe_hbm, ke_hbm,
    qg_ref, kg_ref,
    count_ref, krecv, kother, qrecv, qother, e_buf, s_buf, piece_stats, st_send, st_recv,
    kg_send, kg_recv, qg_send, qg_recv, qg_own,
    load_sem, ksend_sem, krecv_sem, qsend_sem, qrecv_sem, st_sems,
    kgsend_sem, kgrecv_sem, qgsend_sem, qgrecv_sem,
):
    members = chips // 2
    rows = krecv.shape[3]
    all_rows = rows * chips * 2
    text_slots = min(512, all_rows // 4)
    scale = 1.0 / math.sqrt(HEAD_DIM)
    weight = 4.0 * all_rows * math.sqrt(all_rows)
    me = lax.axis_index("ctx")
    chip, core = me // 2, me % 2
    other = 1 - core

    if SQUARE:
        group, member = chip // members, chip % members
        chip_of = lambda g, m: g * members + m
    else:
        group, member = chip % 2, chip // 2
        chip_of = lambda g, m: m * 2 + g

    def dev(g, m, c):
        return {"ctx": chip_of(g, m) * 2 + c}

    def shifted(d):
        if members % 2:
            return (member + d) % members
        return (member // 2 + d // 2) % (members // 2) * 2 + (member + d) % 2

    def sender(d):
        if members % 2:
            return (member + members - d) % members
        return (member // 2 + members - d // 2) % (members // 2) * 2 + (member + d) % 2

    def each(n, body, init):
        if n <= 8:
            for i in range(n):
                init = body(i, init)
            return init
        return lax.fori_loop(0, n, body, init)

    own_cols = pl.ds(pl.multiple_of(core * HEAD_DIM, HEAD_DIM), HEAD_DIM)
    other_cols = pl.ds(pl.multiple_of(other * HEAD_DIM, HEAD_DIM), HEAD_DIM)
    loads = []
    for i, (src, dst_own, dst_other) in enumerate((
        (ks_hbm, krecv.at[member, core, 0], kother.at[0]),
        (ke_hbm, krecv.at[member, core, 1], kother.at[1]),
        (qs_hbm, qrecv.at[group, core, 0], qother.at[0]),
        (qe_hbm, qrecv.at[group, core, 1], qother.at[1]),
    )):
        loads.append(pltpu.make_async_copy(src.at[:, own_cols], dst_own, load_sem.at[2 * i]))
        loads.append(pltpu.make_async_copy(src.at[:, other_cols], dst_other, load_sem.at[2 * i + 1]))
    loads.append(pltpu.make_async_copy(count_hbm, count_ref, load_sem.at[8]))
    for load in loads:
        load.start()

    barrier = pltpu.get_barrier_semaphore()

    def greet(d, carry):
        for c in (0, 1):
            pl.semaphore_signal(barrier, inc=1, device_id=dev(group, shifted(d + 1), c))
        return carry

    for c in (0, 1):
        pl.semaphore_signal(barrier, inc=1, device_id=dev(1 - group, member, c))
    pl.semaphore_signal(barrier, inc=1, device_id=dev(group, member, other))
    each(members - 1, greet, 0)
    pl.semaphore_wait(barrier, 2 * members + 1)
    for load in loads:
        load.wait()

    def key_copy(m, c, same):
        return pltpu.make_async_remote_copy(
            src_ref=krecv.at[member, core] if same else kother,
            dst_ref=krecv.at[member, core],
            send_sem=ksend_sem.at[m, c],
            recv_sem=krecv_sem.at[member, core],
            device_id=dev(group, m, c),
        )

    def key_arrival(m, c):
        return pltpu.make_async_remote_copy(
            src_ref=kother,
            dst_ref=krecv.at[m, c],
            send_sem=ksend_sem.at[m, c],
            recv_sem=krecv_sem.at[m, c],
            device_id=dev(group, m, c),
        )

    def query_copy(g, c, same):
        return pltpu.make_async_remote_copy(
            src_ref=qrecv.at[group, core] if same else qother,
            dst_ref=qrecv.at[group, core],
            send_sem=qsend_sem.at[g, c],
            recv_sem=qrecv_sem.at[group, core],
            device_id=dev(g, member, c),
        )

    def query_arrival(g, c):
        return pltpu.make_async_remote_copy(
            src_ref=qother,
            dst_ref=qrecv.at[g, c],
            send_sem=qsend_sem.at[g, c],
            recv_sem=qrecv_sem.at[g, c],
            device_id=dev(g, member, c),
        )

    query_copy(1 - group, core, True).start()
    query_copy(1 - group, other, False).start()
    query_copy(group, other, False).start()
    key_copy(member, other, False).start()

    def send_keys(d, carry):
        m = shifted(members - 1 - d)
        key_copy(m, core, True).start()
        key_copy(m, other, False).start()
        return carry

    each(members - 1, send_keys, 0)

    count = count_ref[0]

    def valid(positions):
        return (positions >= text_slots) | (positions < count)

    query_arrival(group, other).wait_recv()
    query_arrival(1 - group, core).wait_recv()
    query_arrival(1 - group, other).wait_recv()

    def queries(which):
        pieces = [qrecv[g, c, which].astype(F32) for g in (0, 1) for c in (0, 1)]
        return jnp.concatenate(pieces, axis=0).astype(BF16)

    q_source, q_edit = queries(0), queries(1)
    width = 4 * rows
    lane = lax.broadcasted_iota(jnp.int32, (1, width), 1)
    piece = lane // rows
    lane_chip = jnp.where(piece < 2, chip_of(0, member), chip_of(1, member))
    row_place = (lane_chip * 2 + piece % 2) * rows + lane % rows
    row_weight = jnp.where(valid(row_place), 2.0 * weight, 0.0)

    def merge(a, b):
        me1, le1, ms1, ls1, sq1, cr1 = a
        me2, le2, ms2, ls2, sq2, cr2 = b
        m_e, m_s = jnp.maximum(me1, me2), jnp.maximum(ms1, ms2)
        fe1, fe2 = jnp.exp(me1 - m_e), jnp.exp(me2 - m_e)
        fs1, fs2 = jnp.exp(ms1 - m_s), jnp.exp(ms2 - m_s)
        return (
            m_e, le1 * fe1 + le2 * fe2,
            m_s, ls1 * fs1 + ls2 * fs2,
            sq1 * fe1 * fe1 + sq2 * fe2 * fe2,
            cr1 * fe1 * fs1 + cr2 * fe2 * fs2,
        )

    def powers(k, keys, q, key_valid, buf):
        scores = lax.dot_general(
            keys, q, (((1,), (1,)), ((), ())), preferred_element_type=F32
        ) * scale
        scores = jnp.where(key_valid, scores, MASKED)
        top = jnp.max(scores, axis=0, keepdims=True)
        power = jnp.where(key_valid, jnp.exp(scores - top), 0.0)
        buf[k] = power
        return top, power, jnp.sum(power, axis=0, keepdims=True)

    def score_piece(k, m, c):
        place = (chip_of(group, m) * 2 + c) * rows + lax.broadcasted_iota(jnp.int32, (rows, 1), 0)
        key_valid = valid(place)
        m_s, s_pow, l_s = powers(k, krecv[m, c, 0], q_source, key_valid, s_buf)
        m_e, e_pow, l_e = powers(k, krecv[m, c, 1], q_edit, key_valid, e_buf)
        sq = jnp.sum(e_pow * e_pow, axis=0, keepdims=True)
        cr = jnp.sum(e_pow * s_pow, axis=0, keepdims=True)
        for i, value in enumerate((m_e, l_e, m_s, l_s, sq, cr)):
            piece_stats[i, pl.ds(k, 1)] = value

    score_piece(0, member, core)
    key_arrival(member, other).wait_recv()
    score_piece(1, member, other)

    def far_scores(d, carry):
        m = sender(d + 1)
        for i, c in enumerate((core, other)):
            key_arrival(m, c).wait_recv()
            score_piece(2 * (d + 1) + i, m, c)
        return carry

    each(members - 1, far_scores, 0)
    tops_e, tops_s = piece_stats[0], piece_stats[2]
    m_e, m_s = jnp.max(tops_e, axis=0, keepdims=True), jnp.max(tops_s, axis=0, keepdims=True)
    f_e, f_s = jnp.exp(tops_e - m_e), jnp.exp(tops_s - m_s)
    stats = (
        m_e, jnp.sum(piece_stats[1] * f_e, axis=0, keepdims=True),
        m_s, jnp.sum(piece_stats[3] * f_s, axis=0, keepdims=True),
        jnp.sum(piece_stats[4] * (f_e * f_e), axis=0, keepdims=True),
        jnp.sum(piece_stats[5] * (f_e * f_s), axis=0, keepdims=True),
    )

    for i, value in enumerate(stats):
        st_send[i:i + 1] = value
    for i in (6, 7):
        st_send[i:i + 1] = jnp.zeros((1, width), F32)
    stat_copy = pltpu.make_async_remote_copy(
        src_ref=st_send, dst_ref=st_recv, send_sem=st_sems.at[0], recv_sem=st_sems.at[1],
        device_id=dev(1 - group, member, core),
    )
    stat_copy.start()
    stat_copy.wait_recv()
    m_e, l_e, m_s, l_s, sq, cr = merge(stats, tuple(st_recv[i:i + 1] for i in range(6)))
    inv_e, inv_s = 1.0 / l_e, 1.0 / l_s
    piece_stats[1] = jnp.exp(tops_e - m_e) * inv_e
    piece_stats[3] = jnp.exp(tops_s - m_s) * inv_s
    delta = row_weight * (sq * inv_e * inv_e - cr * inv_e * inv_s)

    def kg_copy(m, c):
        return pltpu.make_async_remote_copy(
            src_ref=kg_send.at[m, c], dst_ref=kg_recv.at[member, core],
            send_sem=kgsend_sem.at[m, c], recv_sem=kgrecv_sem.at[member, core],
            device_id=dev(group, m, c),
        )

    def kg_arrival(m, c):
        return pltpu.make_async_remote_copy(
            src_ref=kg_send.at[m, c], dst_ref=kg_recv.at[m, c],
            send_sem=kgsend_sem.at[m, c], recv_sem=kgrecv_sem.at[m, c],
            device_id=dev(group, m, c),
        )

    def qg_copy(g, c):
        return pltpu.make_async_remote_copy(
            src_ref=qg_send.at[g, c], dst_ref=qg_recv.at[group, core],
            send_sem=qgsend_sem.at[g, c], recv_sem=qgrecv_sem.at[group, core],
            device_id=dev(g, member, c),
        )

    def qg_arrival(g, c):
        return pltpu.make_async_remote_copy(
            src_ref=qg_send.at[g, c], dst_ref=qg_recv.at[g, c],
            send_sem=qgsend_sem.at[g, c], recv_sem=qgrecv_sem.at[g, c],
            device_id=dev(g, member, c),
        )

    def grad_chunk(d, m, q_total):
        grads, keys = [], []
        for i, c in enumerate((core, other)):
            k = 2 * d + i
            prob_e = e_buf[k] * piece_stats[1, pl.ds(k, 1)]
            prob_s = s_buf[k] * piece_stats[3, pl.ds(k, 1)]
            grads.append(prob_e * (row_weight * (prob_e - prob_s) - delta))
            keys.append(krecv[m, c, 1].astype(F32))
        grad = jnp.concatenate(grads, axis=0).astype(BF16)
        k_part = jnp.dot(grad, q_edit, preferred_element_type=F32) * scale
        q_part = lax.dot_general(
            jnp.concatenate(keys, axis=0).astype(BF16), grad,
            (((0,), (0,)), ((), ())), preferred_element_type=F32,
        )
        return k_part, q_part if q_total is None else q_total + q_part

    def far_grad(d, q_total):
        d = members - 1 - d
        m = sender(d)
        k_part, q_total = grad_chunk(d, m, q_total)
        for i, c in enumerate((core, other)):
            kg_send[m, c] = k_part[i * rows:(i + 1) * rows].astype(BF16)
            kg_copy(m, c).start()
        return q_total

    q_total = each(members - 1, far_grad, jnp.zeros((HEAD_DIM, width), F32))
    k_part, q_total = grad_chunk(0, member, q_total)
    kg_mine = k_part[:rows]
    kg_send[member, other] = k_part[rows:].astype(BF16)
    kg_copy(member, other).start()

    q_rows = q_total.T * scale
    for g in (0, 1):
        for c in (0, 1):
            part = q_rows[(2 * g + c) * rows:(2 * g + c + 1) * rows]
            qg_own[g, c] = part
            qg_send[g, c] = part.astype(BF16)
    qg_copy(1 - group, core).start()
    qg_copy(1 - group, other).start()
    qg_copy(group, other).start()

    def put(ref, mine, theirs):
        ref[:, :HEAD_DIM] = jnp.where(core == 0, mine, theirs)
        ref[:, HEAD_DIM:] = jnp.where(core == 0, theirs, mine)

    kg_arrival(member, other).wait_recv()

    def add_far(d, sums):
        mine, theirs = sums
        m = shifted(d + 1)
        kg_arrival(m, core).wait_recv()
        kg_arrival(m, other).wait_recv()
        return mine + kg_recv[m, core].astype(F32), theirs + kg_recv[m, other].astype(F32)

    sums = each(members - 1, add_far, (kg_mine, kg_recv[member, other].astype(F32)))
    put(kg_ref, *sums)

    qg_arrival(group, other).wait_recv()
    qg_arrival(1 - group, core).wait_recv()
    qg_arrival(1 - group, other).wait_recv()
    put(
        qg_ref,
        qg_own[group, core] + qg_recv[1 - group, core].astype(F32),
        qg_recv[group, other].astype(F32) + qg_recv[1 - group, other].astype(F32),
    )

    def drain(d, carry):
        m = shifted(d + 1)
        for c in (0, 1):
            key_copy(m, c, False).wait_send()
            kg_copy(m, c).wait_send()
        return carry

    each(members - 1, drain, 0)
    key_copy(member, other, False).wait_send()
    kg_copy(member, other).wait_send()
    for copy in (query_copy(1 - group, core, True), query_copy(1 - group, other, False),
                 query_copy(group, other, False), qg_copy(1 - group, core),
                 qg_copy(1 - group, other), qg_copy(group, other), stat_copy):
        copy.wait_send()


def put_out(qg_vmem, kg_vmem, qg_hbm, kg_hbm, sems):
    copies = (
        pltpu.make_async_copy(qg_vmem, qg_hbm, sems.at[0]),
        pltpu.make_async_copy(kg_vmem, kg_hbm, sems.at[1]),
    )
    for copy in copies:
        copy.start()
    for copy in copies:
        copy.wait()


def solution(mesh):
    chips = mesh.shape["ctx"] // 2
    members = chips // 2

    def local(query_source, key_source, query_edit, key_edit, text_count):
        rows, full = query_source.shape
        width = 4 * rows
        dma = pltpu.SemaphoreType.DMA
        vmem = pltpu.VMEM
        any_spec = pl.BlockSpec(memory_space=pl.ANY)
        grads = pl.pallas_call(
            functools.partial(kernel, chips),
            out_shape=(
                pltpu.VMEM((rows, full), F32),
                pltpu.VMEM((rows, full), F32),
            ),
            in_specs=[pl.BlockSpec(memory_space=pltpu.HBM)] * 5,
            out_specs=(pl.BlockSpec(memory_space=pltpu.VMEM),) * 2,
            scratch_shapes=[
                pltpu.SMEM((1,), jnp.int32),
                vmem((members, 2, 2, rows, HEAD_DIM), BF16),
                vmem((2, rows, HEAD_DIM), BF16),
                vmem((2, 2, 2, rows, HEAD_DIM), BF16),
                vmem((2, rows, HEAD_DIM), BF16),
                vmem((2 * members, rows, width), F32),
                vmem((2 * members, rows, width), F32),
                vmem((6, 2 * members, width), F32),
                vmem((8, width), F32),
                vmem((8, width), F32),
                vmem((members, 2, rows, HEAD_DIM), BF16),
                vmem((members, 2, rows, HEAD_DIM), BF16),
                vmem((2, 2, rows, HEAD_DIM), BF16),
                vmem((2, 2, rows, HEAD_DIM), BF16),
                vmem((2, 2, rows, HEAD_DIM), F32),
                dma((9,)),
                dma((members, 2)),
                dma((members, 2)),
                dma((2, 2)),
                dma((2, 2)),
                dma((2,)),
                dma((members, 2)),
                dma((members, 2)),
                dma((2, 2)),
                dma((2, 2)),
            ],
            compiler_params=pltpu.CompilerParams(collective_id=0, has_side_effects=True),
        )(text_count, query_source, key_source, query_edit, key_edit)
        return pl.pallas_call(
            put_out,
            out_shape=(pltpu.HBM((rows, full), F32),) * 2,
            in_specs=[pl.BlockSpec(memory_space=pltpu.VMEM)] * 2,
            out_specs=(pl.BlockSpec(memory_space=pltpu.HBM),) * 2,
            scratch_shapes=[dma((2,))],
        )(*(pltpu.with_memory_space_constraint(g, pltpu.VMEM) for g in grads))

    spec = P(("req", "ctx"), None)
    return jax.shard_map(
        local, mesh=mesh, in_specs=(spec,) * 4 + (P("req"),), out_specs=(spec, spec), check_vma=False
    )
```

```python
import functools
import math

import jax
import jax.numpy as jnp
from jax import lax
from jax.experimental import pallas as pl
from jax.experimental.pallas import tpu as pltpu
from jax.sharding import PartitionSpec as P

HEAD_DIM = 128
MASKED = -1e30
SQUARE = True
F32 = jnp.float32
BF16 = jnp.bfloat16


def kernel(
    chips,
    count_hbm, qs_hbm, ks_hbm, qe_hbm, ke_hbm,
    qg_ref, kg_ref,
    count_ref, krecv, kother, qrecv, qother, e_buf, s_buf, piece_stats, st_send, st_recv,
    kg_send, kg_recv, qg_send, qg_recv, qg_own,
    load_sem, ksend_sem, krecv_sem, qsend_sem, qrecv_sem, st_sems,
    kgsend_sem, kgrecv_sem, qgsend_sem, qgrecv_sem,
):
    members = chips // 2
    rows = krecv.shape[3]
    all_rows = rows * chips * 2
    text_slots = min(512, all_rows // 4)
    scale = 1.0 / math.sqrt(HEAD_DIM)
    weight = 4.0 * all_rows * math.sqrt(all_rows)
    me = lax.axis_index("ctx")
    chip, core = me // 2, me % 2
    other = 1 - core

    if SQUARE:
        group, member = chip // members, chip % members
        chip_of = lambda g, m: g * members + m
    else:
        group, member = chip % 2, chip // 2
        chip_of = lambda g, m: m * 2 + g

    def dev(g, m, c):
        return {"ctx": chip_of(g, m) * 2 + c}

    def shifted(d):
        if members % 2:
            return (member + d) % members
        return (member // 2 + d // 2) % (members // 2) * 2 + (member + d) % 2

    def cycled(d):
        return (member + d) % members

    def sender(d):
        if members % 2:
            return (member + members - d) % members
        return (member // 2 + members - d // 2) % (members // 2) * 2 + (member + d) % 2

    def each(n, body, init):
        if n <= 8:
            for i in range(n):
                init = body(i, init)
            return init
        return lax.fori_loop(0, n, body, init)

    own_cols = pl.ds(pl.multiple_of(core * HEAD_DIM, HEAD_DIM), HEAD_DIM)
    other_cols = pl.ds(pl.multiple_of(other * HEAD_DIM, HEAD_DIM), HEAD_DIM)
    loads = []
    for i, (src, dst_own, dst_other) in enumerate((
        (ks_hbm, krecv.at[member, core, 0], kother.at[0]),
        (ke_hbm, krecv.at[member, core, 1], kother.at[1]),
        (qs_hbm, qrecv.at[group, core, 0], qother.at[0]),
        (qe_hbm, qrecv.at[group, core, 1], qother.at[1]),
    )):
        loads.append(pltpu.make_async_copy(src.at[:, own_cols], dst_own, load_sem.at[2 * i]))
        loads.append(pltpu.make_async_copy(src.at[:, other_cols], dst_other, load_sem.at[2 * i + 1]))
    loads.append(pltpu.make_async_copy(count_hbm, count_ref, load_sem.at[8]))
    for load in loads:
        load.start()

    barrier = pltpu.get_barrier_semaphore()

    def greet(d, carry):
        for c in (0, 1):
            pl.semaphore_signal(barrier, inc=1, device_id=dev(group, shifted(d + 1), c))
        return carry

    for c in (0, 1):
        pl.semaphore_signal(barrier, inc=1, device_id=dev(1 - group, member, c))
    pl.semaphore_signal(barrier, inc=1, device_id=dev(group, member, other))
    each(members - 1, greet, 0)
    pl.semaphore_wait(barrier, 2 * members + 1)
    for load in loads:
        load.wait()

    def key_copy(m, c, same):
        return pltpu.make_async_remote_copy(
            src_ref=krecv.at[member, core] if same else kother,
            dst_ref=krecv.at[member, core],
            send_sem=ksend_sem.at[m, c],
            recv_sem=krecv_sem.at[member, core],
            device_id=dev(group, m, c),
        )

    def key_arrival(m, c):
        return pltpu.make_async_remote_copy(
            src_ref=kother,
            dst_ref=krecv.at[m, c],
            send_sem=ksend_sem.at[m, c],
            recv_sem=krecv_sem.at[m, c],
            device_id=dev(group, m, c),
        )

    def query_copy(g, c, same):
        return pltpu.make_async_remote_copy(
            src_ref=qrecv.at[group, core] if same else qother,
            dst_ref=qrecv.at[group, core],
            send_sem=qsend_sem.at[g, c],
            recv_sem=qrecv_sem.at[group, core],
            device_id=dev(g, member, c),
        )

    def query_arrival(g, c):
        return pltpu.make_async_remote_copy(
            src_ref=qother,
            dst_ref=qrecv.at[g, c],
            send_sem=qsend_sem.at[g, c],
            recv_sem=qrecv_sem.at[g, c],
            device_id=dev(g, member, c),
        )

    query_copy(1 - group, core, True).start()
    query_copy(1 - group, other, False).start()
    query_copy(group, other, False).start()
    key_copy(member, other, False).start()

    def send_keys(d, carry):
        m = cycled(d + 1)
        key_copy(m, core, True).start()
        key_copy(m, other, False).start()
        return carry

    each(members - 1, send_keys, 0)

    count = count_ref[0]

    def valid(positions):
        return (positions >= text_slots) | (positions < count)

    query_arrival(group, other).wait_recv()
    query_arrival(1 - group, core).wait_recv()
    query_arrival(1 - group, other).wait_recv()

    def queries(which):
        pieces = [qrecv[g, c, which].astype(F32) for g in (0, 1) for c in (0, 1)]
        return jnp.concatenate(pieces, axis=0).astype(BF16)

    q_source, q_edit = queries(0), queries(1)
    width = 4 * rows
    lane = lax.broadcasted_iota(jnp.int32, (1, width), 1)
    piece = lane // rows
    lane_chip = jnp.where(piece < 2, chip_of(0, member), chip_of(1, member))
    row_place = (lane_chip * 2 + piece % 2) * rows + lane % rows
    row_weight = jnp.where(valid(row_place), 2.0 * weight, 0.0)

    def merge(a, b):
        me1, le1, ms1, ls1, sq1, cr1 = a
        me2, le2, ms2, ls2, sq2, cr2 = b
        m_e, m_s = jnp.maximum(me1, me2), jnp.maximum(ms1, ms2)
        fe1, fe2 = jnp.exp2(me1 - m_e), jnp.exp2(me2 - m_e)
        fs1, fs2 = jnp.exp2(ms1 - m_s), jnp.exp2(ms2 - m_s)
        return (
            m_e, le1 * fe1 + le2 * fe2,
            m_s, ls1 * fs1 + ls2 * fs2,
            sq1 * fe1 * fe1 + sq2 * fe2 * fe2,
            cr1 * fe1 * fs1 + cr2 * fe2 * fs2,
        )

    def powers(k, keys, q, key_valid, buf):
        scores = lax.dot_general(
            keys, q, (((1,), (1,)), ((), ())), preferred_element_type=F32
        ) * (scale * math.log2(math.e))
        scores = jnp.where(key_valid, scores, MASKED)
        top = jnp.max(scores, axis=0, keepdims=True)
        power = jnp.exp2(scores - top)
        buf[k] = power
        return top, power, jnp.sum(power, axis=0, keepdims=True)

    def score_piece(k, m, c):
        place = (chip_of(group, m) * 2 + c) * rows + lax.broadcasted_iota(jnp.int32, (rows, 1), 0)
        key_valid = valid(place)
        m_s, s_pow, l_s = powers(k, krecv[m, c, 0], q_source, key_valid, s_buf)
        m_e, e_pow, l_e = powers(k, krecv[m, c, 1], q_edit, key_valid, e_buf)
        sq = jnp.sum(e_pow * e_pow, axis=0, keepdims=True)
        cr = jnp.sum(e_pow * s_pow, axis=0, keepdims=True)
        for i, value in enumerate((m_e, l_e, m_s, l_s, sq, cr)):
            piece_stats[i, pl.ds(k, 1)] = value

    score_piece(0, member, core)
    key_arrival(member, other).wait_recv()
    score_piece(1, member, other)

    def far_scores(d, carry):
        m = cycled(members - 1 - d)
        for c in (core, other):
            key_arrival(m, c).wait_recv()
        for i, c in enumerate((core, other)):
            score_piece(2 * (d + 1) + i, m, c)
        return carry

    each(members - 1, far_scores, 0)
    tops_e, tops_s = piece_stats[0], piece_stats[2]
    m_e, m_s = jnp.max(tops_e, axis=0, keepdims=True), jnp.max(tops_s, axis=0, keepdims=True)
    f_e, f_s = jnp.exp2(tops_e - m_e), jnp.exp2(tops_s - m_s)
    stats = (
        m_e, jnp.sum(piece_stats[1] * f_e, axis=0, keepdims=True),
        m_s, jnp.sum(piece_stats[3] * f_s, axis=0, keepdims=True),
        jnp.sum(piece_stats[4] * (f_e * f_e), axis=0, keepdims=True),
        jnp.sum(piece_stats[5] * (f_e * f_s), axis=0, keepdims=True),
    )

    for i, value in enumerate(stats):
        st_send[i:i + 1] = value
    for i in (6, 7):
        st_send[i:i + 1] = jnp.zeros((1, width), F32)
    stat_copy = pltpu.make_async_remote_copy(
        src_ref=st_send, dst_ref=st_recv, send_sem=st_sems.at[0], recv_sem=st_sems.at[1],
        device_id=dev(1 - group, member, core),
    )
    stat_copy.start()
    stat_copy.wait_recv()
    m_e, l_e, m_s, l_s, sq, cr = merge(stats, tuple(st_recv[i:i + 1] for i in range(6)))
    inv_e, inv_s = 1.0 / l_e, 1.0 / l_s
    piece_stats[1] = jnp.exp2(tops_e - m_e) * inv_e
    piece_stats[3] = jnp.exp2(tops_s - m_s) * inv_s
    delta = row_weight * (sq * inv_e * inv_e - cr * inv_e * inv_s)

    def kg_copy(m, c):
        return pltpu.make_async_remote_copy(
            src_ref=kg_send.at[m, c], dst_ref=kg_recv.at[member, core],
            send_sem=kgsend_sem.at[m, c], recv_sem=kgrecv_sem.at[member, core],
            device_id=dev(group, m, c),
        )

    def kg_arrival(m, c):
        return pltpu.make_async_remote_copy(
            src_ref=kg_send.at[m, c], dst_ref=kg_recv.at[m, c],
            send_sem=kgsend_sem.at[m, c], recv_sem=kgrecv_sem.at[m, c],
            device_id=dev(group, m, c),
        )

    def qg_copy(g, c):
        return pltpu.make_async_remote_copy(
            src_ref=qg_send.at[g, c], dst_ref=qg_recv.at[group, core],
            send_sem=qgsend_sem.at[g, c], recv_sem=qgrecv_sem.at[group, core],
            device_id=dev(g, member, c),
        )

    def qg_arrival(g, c):
        return pltpu.make_async_remote_copy(
            src_ref=qg_send.at[g, c], dst_ref=qg_recv.at[g, c],
            send_sem=qgsend_sem.at[g, c], recv_sem=qgrecv_sem.at[g, c],
            device_id=dev(g, member, c),
        )

    def grad_chunk(d, m, q_total):
        grads, keys = [], []
        for i, c in enumerate((core, other)):
            k = 2 * d + i
            prob_e = e_buf[k] * piece_stats[1, pl.ds(k, 1)]
            prob_s = s_buf[k] * piece_stats[3, pl.ds(k, 1)]
            grads.append(prob_e * (row_weight * (prob_e - prob_s) - delta))
            keys.append(krecv[m, c, 1].astype(F32))
        grad = jnp.concatenate(grads, axis=0).astype(BF16)
        k_part = jnp.dot(grad, q_edit, preferred_element_type=F32) * scale
        q_part = lax.dot_general(
            jnp.concatenate(keys, axis=0).astype(BF16), grad,
            (((0,), (0,)), ((), ())), preferred_element_type=F32,
        )
        return k_part, q_part if q_total is None else q_total + q_part

    def far_grad(d, q_total):
        d = members - 1 - d
        m = cycled(members - d)
        k_part, q_total = grad_chunk(d, m, q_total)
        for i, c in enumerate((core, other)):
            kg_send[m, c] = k_part[i * rows:(i + 1) * rows].astype(BF16)
        return q_total

    q_total = each(members - 1, far_grad, jnp.zeros((HEAD_DIM, width), F32))
    k_part, q_total = grad_chunk(0, member, q_total)
    kg_mine = k_part[:rows]
    kg_send[member, other] = k_part[rows:].astype(BF16)

    q_rows = q_total.T * scale
    for g in (0, 1):
        for c in (0, 1):
            part = q_rows[(2 * g + c) * rows:(2 * g + c + 1) * rows]
            qg_own[g, c] = part
            qg_send[g, c] = part.astype(BF16)
    qg_copy(1 - group, core).start()
    qg_copy(1 - group, other).start()
    qg_copy(group, other).start()

    def send_kg(d, carry):
        m = cycled(members - 1 - d)
        for c in (core, other):
            kg_copy(m, c).start()
        return carry

    each(members - 1, send_kg, 0)
    kg_copy(member, other).start()

    def put(ref, mine, theirs):
        ref[:, :HEAD_DIM] = jnp.where(core == 0, mine, theirs)
        ref[:, HEAD_DIM:] = jnp.where(core == 0, theirs, mine)

    kg_arrival(member, other).wait_recv()

    def add_far(d, sums):
        mine, theirs = sums
        m = shifted(d + 1)
        kg_arrival(m, core).wait_recv()
        kg_arrival(m, other).wait_recv()
        return mine + kg_recv[m, core].astype(F32), theirs + kg_recv[m, other].astype(F32)

    sums = each(members - 1, add_far, (kg_mine, kg_recv[member, other].astype(F32)))
    put(kg_ref, *sums)

    qg_arrival(group, other).wait_recv()
    qg_arrival(1 - group, core).wait_recv()
    qg_arrival(1 - group, other).wait_recv()
    put(
        qg_ref,
        qg_own[group, core] + qg_recv[1 - group, core].astype(F32),
        qg_recv[group, other].astype(F32) + qg_recv[1 - group, other].astype(F32),
    )

    def drain(d, carry):
        m = shifted(d + 1)
        for c in (0, 1):
            key_copy(m, c, False).wait_send()
            kg_copy(m, c).wait_send()
        return carry

    each(members - 1, drain, 0)
    key_copy(member, other, False).wait_send()
    kg_copy(member, other).wait_send()
    for copy in (query_copy(1 - group, core, True), query_copy(1 - group, other, False),
                 query_copy(group, other, False), qg_copy(1 - group, core),
                 qg_copy(1 - group, other), qg_copy(group, other), stat_copy):
        copy.wait_send()


def put_out(qg_vmem, kg_vmem, qg_hbm, kg_hbm, sems):
    copies = (
        pltpu.make_async_copy(qg_vmem, qg_hbm, sems.at[0]),
        pltpu.make_async_copy(kg_vmem, kg_hbm, sems.at[1]),
    )
    for copy in copies:
        copy.start()
    for copy in copies:
        copy.wait()


def solution(mesh):
    chips = mesh.shape["ctx"] // 2
    members = chips // 2

    def local(query_source, key_source, query_edit, key_edit, text_count):
        rows, full = query_source.shape
        width = 4 * rows
        dma = pltpu.SemaphoreType.DMA
        vmem = pltpu.VMEM
        any_spec = pl.BlockSpec(memory_space=pl.ANY)
        grads = pl.pallas_call(
            functools.partial(kernel, chips),
            out_shape=(
                pltpu.VMEM((rows, full), F32),
                pltpu.VMEM((rows, full), F32),
            ),
            in_specs=[pl.BlockSpec(memory_space=pltpu.HBM)] * 5,
            out_specs=(pl.BlockSpec(memory_space=pltpu.VMEM),) * 2,
            scratch_shapes=[
                pltpu.SMEM((1,), jnp.int32),
                vmem((members, 2, 2, rows, HEAD_DIM), BF16),
                vmem((2, rows, HEAD_DIM), BF16),
                vmem((2, 2, 2, rows, HEAD_DIM), BF16),
                vmem((2, rows, HEAD_DIM), BF16),
                vmem((2 * members, rows, width), F32),
                vmem((2 * members, rows, width), F32),
                vmem((6, 2 * members, width), F32),
                vmem((8, width), F32),
                vmem((8, width), F32),
                vmem((members, 2, rows, HEAD_DIM), BF16),
                vmem((members, 2, rows, HEAD_DIM), BF16),
                vmem((2, 2, rows, HEAD_DIM), BF16),
                vmem((2, 2, rows, HEAD_DIM), BF16),
                vmem((2, 2, rows, HEAD_DIM), F32),
                dma((9,)),
                dma((members, 2)),
                dma((members, 2)),
                dma((2, 2)),
                dma((2, 2)),
                dma((2,)),
                dma((members, 2)),
                dma((members, 2)),
                dma((2, 2)),
                dma((2, 2)),
            ],
            compiler_params=pltpu.CompilerParams(collective_id=0, has_side_effects=True),
        )(text_count, query_source, key_source, query_edit, key_edit)
        return pl.pallas_call(
            put_out,
            out_shape=(pltpu.HBM((rows, full), F32),) * 2,
            in_specs=[pl.BlockSpec(memory_space=pltpu.VMEM)] * 2,
            out_specs=(pl.BlockSpec(memory_space=pltpu.HBM),) * 2,
            scratch_shapes=[dma((2,))],
        )(*(pltpu.with_memory_space_constraint(g, pltpu.VMEM) for g in grads))

    spec = P(("req", "ctx"), None)
    return jax.shard_map(
        local, mesh=mesh, in_specs=(spec,) * 4 + (P("req"),), out_specs=(spec, spec), check_vma=False
    )
```
